128 devices in a mesh: wide: 32 (over y, x, core), col: 4 (over z).
Axes of the slice: x: 4, y: 4, z: 4, core: 2. Of those that a mesh axis runs over, the one named last changes fastest.
Arguments:
- coeffs: float32 [512, 512], P('wide'), may hold values from -6 to 6
- pod_basis: float32 [512, 512, 1024], P(None, 'wide', 'col'), may hold values from -0.5 to 0.5
- mean_field: float32 [512, 1024], P('wide', 'col'), may hold values from -3 to 3
- velocity: float32 [2, 512, 1024], P(None, 'wide', 'col'), may hold values from -1 to 1
- diffusivity: float32 [512, 1024], P('wide', 'col'), may hold values from 0.05 to 0.3
- reaction: float32 [512, 1024], P('wide', 'col'), may hold values from 0.2 to 2
Outputs:
- advanced: float32 [512, 512], P('wide')
- mean_rate: float32 [512, 512], P('wide')
The draws below stay inside these ranges and needn't reach their ends.
All inputs are finite; a program needn't handle non-finite values. Where the reference program divides by a largest or mean magnitude, that divisor is 1e-20 or more.
Results may differ from the reference program's by a relative error of at most 0.000068.
Values sent between devices are 32-bit elements; how exact they have to be, the bound alone decides.
A program may use at most 192 MiB of HBM per device.

```python
import math
import jax
import jax.numpy as jnp
from jax import lax

MODES = 512
TRAJ = 512
GRID_ROWS = 512
GRID_COLS = 1024


def raised(entries, key, source, target, parts, factor):
    def block_of(dim):
        return (jnp.arange(entries.shape[dim]) // (entries.shape[dim] // parts)).reshape((-1,) + (1,) * (entries.ndim - 1 - dim))

    one_side = jax.random.permutation(key, parts)[block_of(target)]
    other_side = (block_of(target) + parts // 2) % parts
    return jnp.where((block_of(source) == one_side) | (block_of(source) == other_side), factor * entries, entries)


def levels(stream_key, shape, cuts, low, largest):
    level, own = 1.0, jax.random.fold_in(stream_key, 6)
    for dim, shards_of in cuts:
        steps = jnp.exp(jax.random.uniform(jax.random.fold_in(own, dim), (shards_of,), jnp.float32, low / len(cuts), largest / len(cuts)))
        level = level * jnp.repeat(steps, shape[dim] // shards_of).reshape([-1 if axis == dim else 1 for axis in range(len(shape))])
    return level


def normal_values(stream_key, dims, width, most, pieces=(), kind=jnp.bfloat16):
    array = jax.random.normal(stream_key, dims, jnp.float32) * width
    if len(pieces) > 0:
        array = levels(stream_key, dims, pieces, -0.22, 0.18) * array
    return jnp.clip(array, min=-most, max=most).astype(kind)


def noise_with(rng, dims, width, bound, pieces, heavy, dtype=jnp.bfloat16):
    values = width * jax.random.normal(rng, dims, jnp.float32)
    if pieces:
        values = values * levels(rng, dims, pieces, -0.22, 0.18)
    return jnp.clip(raised(values, jax.random.fold_in(rng, 3), *heavy), -bound, bound).astype(dtype)


def setup_inputs(seed: int = 0) -> dict:
    keys = jax.random.split(jax.random.key(seed), 7)
    coeffs = normal_values(keys[0], (MODES, TRAJ), 1.0, 6.0, ((0, 32),), jnp.float32)
    pod_basis = noise_with(keys[1], (MODES, GRID_ROWS, GRID_COLS), MODES ** -0.5, 0.5, ((1, 32), (2, 4)), (1, 0, 32, 2.75), jnp.float32)
    mean_field = normal_values(keys[2], (GRID_ROWS, GRID_COLS), 0.5, 3.0, ((0, 32), (1, 4)), jnp.float32)
    velocity = jnp.clip(jax.random.uniform(keys[3], (2, GRID_ROWS, GRID_COLS), jnp.float32, -1.0, 1.0) * levels(keys[3], (2, GRID_ROWS, GRID_COLS), ((1, 32), (2, 4)), -0.4, 0.0), -1.0, 1.0)
    diffusivity = jnp.clip(jnp.exp(math.log(0.3) - 1.7917595 * jax.random.uniform(keys[4], (GRID_ROWS, GRID_COLS), jnp.float32) ** levels(keys[4], (GRID_ROWS, GRID_COLS), ((0, 32), (1, 4)), -0.2, 0.2)), 0.05, 0.3)
    reaction = jnp.clip(jnp.exp(math.log(2.0) - 2.3025851 * jax.random.uniform(keys[5], (GRID_ROWS, GRID_COLS), jnp.float32) ** levels(keys[5], (GRID_ROWS, GRID_COLS), ((0, 32), (1, 4)), -0.2, 0.2)), 0.2, 2.0)
    return dict(coeffs=coeffs, pod_basis=pod_basis, mean_field=mean_field, velocity=velocity, diffusivity=diffusivity, reaction=reaction)


highest = lax.Precision.HIGHEST
step_limit = 2.0

def expand_all(flat_basis, mean_cells, coeff_block):
    summed = lax.dot_general(flat_basis, coeff_block, (((0,), (0,)), ((), ())), precision=highest, preferred_element_type=jnp.float32)
    return mean_cells[:, None] + summed

def source_terms(values, velocity, diffusivity, reaction):
    flux_x = velocity[0][:, :, None] * values
    flux_y = velocity[1][:, :, None] * values
    advect = (jnp.roll(flux_x, -1, 0) - jnp.roll(flux_x, 1, 0)) * 0.5 + (jnp.roll(flux_y, -1, 1) - jnp.roll(flux_y, 1, 1)) * 0.5
    laplace = jnp.roll(values, -1, 0) + jnp.roll(values, 1, 0) + jnp.roll(values, -1, 1) + jnp.roll(values, 1, 1) - 4.0 * values
    return -advect + diffusivity[:, :, None] * laplace + reaction[:, :, None] * jnp.tanh(values)

def reference(coeffs, pod_basis, mean_field, velocity, diffusivity, reaction):
    flat_basis = pod_basis.reshape(MODES, GRID_ROWS * GRID_COLS)
    mean_cells = mean_field.reshape(GRID_ROWS * GRID_COLS)
    weight = math.sqrt(MODES / (GRID_ROWS * GRID_COLS))

    def tendency(values_flat):
        grid_values = values_flat.reshape(GRID_ROWS, GRID_COLS, TRAJ)
        source = source_terms(grid_values, velocity, diffusivity, reaction).reshape(GRID_ROWS * GRID_COLS, TRAJ)
        return weight * lax.dot_general(flat_basis, source, (((1,), (0,)), ((), ())), precision=highest, preferred_element_type=jnp.float32)
    field_one = expand_all(flat_basis, mean_cells, coeffs)
    peak_abs = lax.optimization_barrier(jnp.max(jnp.abs(field_one), axis=0))
    step_size = step_limit / (1.0 + peak_abs)
    rate_one = tendency(field_one)
    inter = coeffs + step_size[None, :] * rate_one
    field_two = expand_all(flat_basis, mean_cells, inter)
    rate_two = tendency(field_two)
    mean_rate = (rate_one + rate_two) * 0.5
    advanced = coeffs + step_size[None, :] * mean_rate
    return (advanced, mean_rate)
```

```python
import functools
import math

import jax
import jax.numpy as jnp
from jax import lax
from jax.experimental import pallas as pl
from jax.experimental.pallas import tpu as pltpu
from jax.sharding import PartitionSpec as P

MODES = 512
TRAJ = 512
ROWS = 16
COLS = 256
HALF = 256
PLANE = 16
DEPTH = 4
MESH = pl.DeviceIdType.MESH
F32 = jnp.float32
BF16 = jnp.bfloat16
STEP_LIMIT = 2.0
PAD = 8
ROWPAD = COLS + 2 * PAD
CELLS = ROWS * COLS
EXT = (ROWS + 2) * COLS


def halves(value):
    high = value.astype(BF16)
    return high, (value - high.astype(F32)).astype(BF16)


def kernel(
    weight,
    coeffs, basis, mean, vel, diff, reac,
    adv_out, rate_out,
    stage, bt, bn, ab, mb, field, shi, slo, chi, clo,
    pacc, psum, rcore, rplane, zbuf, cbuf, rate_one, steps,
    edge_rows, halo_rows, edge_cols, halo_cols,
    vrow, mrow, vcol, mcol, kc,
    peak, pcore, pplane, pz,
    load_sem, ag_send, ag_recv, agc_send, agc_recv,
    hal_send, hal_recv, core_send, core_recv, pl_send, pl_recv, z_send, z_recv,
    pkc_send, pkc_recv, pkp_send, pkp_recv, pkz_send, pkz_recv,
):
    wide = lax.axis_index("wide")
    zed = lax.axis_index("col")
    chip = wide // 2
    core = wide % 2
    partner = wide + 1 - 2 * core
    down = (wide + 1) % (2 * PLANE)
    up = (wide + 2 * PLANE - 1) % (2 * PLANE)
    beside = (wide + 2 * PLANE + 2 * core - 1) % (2 * PLANE)

    def plane_peer(i):
        return 2 * ((chip + i) % PLANE) + core

    def load_copy(lt):
        return pltpu.make_async_copy(
            basis.at[:, pl.ds(lt * 128, 128)], stage.at[lt], load_sem.at[lt]
        )

    for lt in range(2):
        load_copy(lt).start()

    barrier = pltpu.get_barrier_semaphore()

    def signal(to_wide, to_zed):
        pl.semaphore_signal(barrier, inc=1, device_id=(to_wide, to_zed), device_id_type=MESH)

    signal(partner, zed)
    signal(beside, zed)

    def greet_plane(i, carry):
        signal(plane_peer(i), zed)
        return carry

    lax.fori_loop(1, PLANE, greet_plane, 0)
    for i in range(1, DEPTH):
        signal(wide, (zed + i) % DEPTH)
    pl.semaphore_wait(barrier, 2 + PLANE - 1 + DEPTH - 1)

    def remote(src, dst, send, recv, to_wide, to_zed):
        return pltpu.make_async_remote_copy(
            src_ref=src, dst_ref=dst, send_sem=send, recv_sem=recv,
            device_id=(to_wide, to_zed), device_id_type=MESH,
        )

    def over_plane(make, act):
        def body(i, carry):
            act(make(i))
            return carry

        lax.fori_loop(1, PLANE, body, 0)

    start = lambda c: c.start()
    wait_recv = lambda c: c.wait_recv()
    wait_send = lambda c: c.wait_send()

    def gather_out(g):
        def make(i):
            own = cbuf.at[g, chip, core]
            return remote(own, own, ag_send.at[g, i], ag_recv.at[g, i], plane_peer(i), zed)

        return make

    def gather_in(g):
        def make(i):
            slot = cbuf.at[g, (chip + PLANE - i) % PLANE, core]
            return remote(slot, slot, ag_send.at[g, i], ag_recv.at[g, i], plane_peer(i), zed)

        return make

    def share_out(g):
        mine = cbuf.at[g, :, core]
        return remote(mine, mine, agc_send.at[g], agc_recv.at[g], partner, zed)

    def share_in(g):
        theirs = cbuf.at[g, :, 1 - core]
        return remote(theirs, theirs, agc_send.at[g], agc_recv.at[g], partner, zed)

    left = (zed + DEPTH - 1) % DEPTH
    right = (zed + 1) % DEPTH
    small = []
    for k, (to_wide, to_zed) in enumerate(((down, zed), (up, zed), (wide, right), (wide, left))):
        if k < 2:
            part = pl.ds(8 * (1 - k), 8)
            small.append(remote(vel.at[0, part, :], vrow.at[k], hal_send.at[0, k], hal_recv.at[0, k], to_wide, to_zed))
            small.append(remote(mean.at[part, :], mrow.at[k], hal_send.at[1, k], hal_recv.at[1, k], to_wide, to_zed))
        else:
            part = pl.ds(128 * (3 - k), 128)
            small.append(remote(vel.at[1, :, part], vcol.at[k - 2], hal_send.at[0, k], hal_recv.at[0, k], to_wide, to_zed))
            small.append(remote(mean.at[:, part], mcol.at[k - 2], hal_send.at[1, k], hal_recv.at[1, k], to_wide, to_zed))
    large = [
        remote(edge_rows.at[0], halo_rows.at[0], hal_send.at[2, 0], hal_recv.at[2, 0], down, zed),
        remote(edge_rows.at[1], halo_rows.at[1], hal_send.at[2, 1], hal_recv.at[2, 1], up, zed),
        remote(edge_cols.at[0], halo_cols.at[0], hal_send.at[2, 2], hal_recv.at[2, 2], wide, right),
        remote(edge_cols.at[1], halo_cols.at[1], hal_send.at[2, 3], hal_recv.at[2, 3], wide, left),
    ]

    for g in range(2):
        cbuf[g, chip, core] = coeffs[:, g * HALF:(g + 1) * HALF]
    over_plane(gather_out(0), start)
    for c in small:
        c.start()
    over_plane(gather_out(1), start)

    for lt in range(2):
        load_copy(lt).wait()

    def prepare(x, q, edge):
        for lt in range(2):
            block = stage[lt, pl.ds(q * (128 * ROWS) + x, 128, stride=ROWS), :]
            high, low = halves(block)
            modes = pl.ds(pl.multiple_of(q * 128, 128), 128)
            lanes = slice(lt * 128, lt * 128 + 128)
            bn[x, modes, lanes] = high
            bn[x, modes, COLS + lt * 128:COLS + lt * 128 + 128] = low
            turned = block.T
            high, low = halves(turned)
            at = pl.ds(pl.multiple_of((x + 1) * COLS + lt * 128, 128), 128)
            bt[at, pl.ds(pl.multiple_of(q * 128, 128), 128)] = high
            bt[at, pl.ds(pl.multiple_of(MODES + q * 128, 128), 128)] = low
            if edge is not None:
                edge_rows[edge, lanes, modes] = turned
            if lt == 0:
                edge_cols[1, x, :, modes] = turned[0:1]
            else:
                edge_cols[0, x, :, modes] = turned[127:128]

    def prepare_edge(x, edge):
        def body(q, carry):
            prepare(x, q, edge)
            return carry

        lax.fori_loop(0, 4, body, 0)

    prepare_edge(ROWS - 1, 0)
    large[0].start()
    prepare_edge(0, 1)
    large[1].start()

    def prepare_inner(k, carry):
        prepare(1 + k // 4, k % 4, None)
        return carry

    lax.fori_loop(0, 4 * (ROWS - 2), prepare_inner, 0)
    large[2].start()
    large[3].start()

    for c in small:
        c.wait_recv()
    vx = vel[0]
    vy = vel[1]
    row_id = lax.broadcasted_iota(jnp.int32, (ROWS, COLS), 0)
    col_id = lax.broadcasted_iota(jnp.int32, (ROWS, COLS), 1)
    vx_next = jnp.where(row_id == ROWS - 1, jnp.broadcast_to(vrow[1, 0:1, :], (ROWS, COLS)), pltpu.roll(vx, ROWS - 1, 0))
    vx_prev = jnp.where(row_id == 0, jnp.broadcast_to(vrow[0, 7:8, :], (ROWS, COLS)), pltpu.roll(vx, 1, 0))
    vy_next = jnp.where(col_id == COLS - 1, jnp.broadcast_to(vcol[1, :, 0:1], (ROWS, COLS)), pltpu.roll(vy, COLS - 1, 1))
    vy_prev = jnp.where(col_id == 0, jnp.broadcast_to(vcol[0, :, 127:128], (ROWS, COLS)), pltpu.roll(vy, 1, 1))
    d = diff[...]
    planes = (d - 0.5 * vx_next, d + 0.5 * vx_prev, d - 0.5 * vy_next, d + 0.5 * vy_prev, -4.0 * d, reac[...], mean[...])
    for k, values in enumerate(planes):
        kc[0:ROWS, k, :] = values
    kc[0:ROWS, 7, :] = jnp.zeros((ROWS, COLS), F32)
    kc[ROWS] = jnp.broadcast_to(mrow[0, 7:8, :], (8, COLS))
    kc[ROWS + 1] = jnp.broadcast_to(mrow[1, 0:1, :], (8, COLS))
    spread = (
        lax.broadcasted_iota(jnp.int32, (8, 7 * 128), 0) == lax.broadcasted_iota(jnp.int32, (8, 7 * 128), 1) // 128
    ).astype(F32)

    def spread_row(x, carry):
        wide_row = lax.dot_general(
            kc[x], spread, (((0,), (0,)), ((), ())), precision=lax.Precision.HIGHEST, preferred_element_type=F32
        )
        for k in range(6):
            ab[k, x] = wide_row[:, k * 128:(k + 1) * 128]
        mb[pl.ds(pl.multiple_of((x + 1) * COLS, COLS), COLS), :] = wide_row[:, 6 * 128:7 * 128]
        return carry

    lax.fori_loop(0, ROWS, spread_row, 0)
    for k, at in ((0, 0), (1, ROWS + 1)):
        wide_row = lax.dot_general(
            kc[ROWS + k], spread[:, 0:128], (((0,), (0,)), ((), ())), precision=lax.Precision.HIGHEST, preferred_element_type=F32
        )
        mb[at * COLS:(at + 1) * COLS, :] = wide_row
    mb[EXT:EXT + 16, :] = jnp.broadcast_to(mcol[0, :, 127:128], (16, 128))
    mb[EXT + 16:EXT + 32, :] = jnp.broadcast_to(mcol[1, :, 0:1], (16, 128))

    def set_coeffs(g):
        high, low = halves(cbuf[g].reshape(MODES, HALF))
        chi[...] = high
        clo[...] = low

    def expand_rows(at, count):
        rows = bt[pl.ds(at, count), :]
        left_side = jnp.concatenate([rows, rows[:, 0:MODES]], axis=1)
        ch = chi[...]
        right_side = jnp.concatenate([ch, ch, clo[...]], axis=0)
        total = jnp.dot(left_side, right_side, preferred_element_type=F32)
        centre = mb[pl.ds(at, count), :]
        return [total[:, lt * 128:(lt + 1) * 128] + centre for lt in range(2)]

    def expand(i):
        at = pl.multiple_of(i * COLS, COLS)
        for lt, values in enumerate(expand_rows(at, COLS)):
            field[lt, i, PAD:PAD + COLS, :] = values

    def expand_sides():
        for lt, values in enumerate(expand_rows(EXT, 32)):
            for x in range(ROWS):
                field[lt, x + 1, PAD - 1:PAD, :] = values[x:x + 1]
                field[lt, x + 1, PAD + COLS:PAD + COLS + 1, :] = values[16 + x:17 + x]

    def source(r, slot, section, h):
        i = r + 1
        for lt in range(2):
            lanes = slice(lt * 128, (lt + 1) * 128)
            here = field[lt, i, PAD:PAD + COLS, :]
            total = ab[0, r] * field[lt, i + 1, PAD:PAD + COLS, :]
            total += ab[1, r] * field[lt, i - 1, PAD:PAD + COLS, :]
            total += ab[2, r] * field[lt, i, PAD + 1:PAD + COLS + 1, :]
            total += ab[3, r] * field[lt, i, PAD - 1:PAD + COLS - 1, :]
            total += ab[4, r] * here
            total += ab[5, r] * jnp.tanh(here)
            high, low = halves(total)
            shi[slot, :, lanes] = high
            slo[slot, :, lanes] = low
            if section == 0:
                tops = jnp.max(jnp.abs(here).reshape(COLS // 8, 8, 128), axis=0)
                peak[h, :, lanes] = jnp.maximum(peak[h, :, lanes], tops)

    def project(r, slot, n):
        sides = bn[r]
        left_side = jnp.concatenate([sides, sides[:, 0:COLS]], axis=1)
        sh = shi[slot]
        right_side = jnp.concatenate([sh, sh, slo[slot]], axis=0)
        part = jnp.dot(left_side, right_side, preferred_element_type=F32)
        pacc[n] = pacc[n] + part.reshape(PLANE, 2, 16, HALF)

    def section_of(section, h, hooks):
        n = 2 * section + h
        expand_sides()
        for i in range(3):
            expand(i)
        pacc[n] = jnp.zeros((PLANE, 2, 16, HALF), F32)
        if section == 0:
            peak[h] = jnp.zeros((8, HALF), F32)
        expand(3)
        source(0, 0, section, h)

        def body(r, carry):
            for at, hook in hooks:
                pl.when(r == at)(hook)
            expand(r + 3)
            source(r, r % 2, section, h)
            project(r - 1, (r - 1) % 2, n)
            return carry

        lax.fori_loop(1, ROWS - 1, body, 0)
        source(ROWS - 1, 1, section, h)
        project(ROWS - 2, 0, n)
        project(ROWS - 1, 1, n)

    def core_out(n):
        return remote(pacc.at[n, :, 1 - core], rcore.at[n], core_send.at[n], core_recv.at[n], partner, zed)

    def peak_core(h):
        return remote(pcore.at[h, 0], pcore.at[h, 1], pkc_send.at[h], pkc_recv.at[h], partner, zed)

    def plane_out(n):
        def make(i):
            return remote(
                psum.at[n, (chip + i) % PLANE], rplane.at[n, i], pl_send.at[n, i], pl_recv.at[n, i], plane_peer(i), zed
            )

        return make

    def peak_plane(h):
        def make(i):
            return remote(pplane.at[h, 0], pplane.at[h, i], pkp_send.at[h, i], pkp_recv.at[h, i], plane_peer(i), zed)

        return make

    def z_out(n, i):
        mine = zbuf.at[n, zed]
        return remote(mine, mine, z_send.at[n, i], z_recv.at[n, i], wide, (zed + i) % DEPTH)

    def z_in(n, i):
        slot = zbuf.at[n, (zed + DEPTH - i) % DEPTH]
        return remote(slot, slot, z_send.at[n, i], z_recv.at[n, i], wide, (zed + i) % DEPTH)

    def peak_z(h, i):
        return remote(pz.at[h, 0], pz.at[h, i], pkz_send.at[h, i], pkz_recv.at[h, i], wide, (zed + i) % DEPTH)

    def sum_start(n):
        core_out(n).start()
        if n < 2:
            pcore[n, 0] = jnp.max(peak[n], axis=0, keepdims=True)
            peak_core(n).start()

    def sum_core(n):
        core_out(n).wait_recv()
        psum[n] = pacc[n, :, core] + rcore[n]
        over_plane(plane_out(n), start)
        if n < 2:
            peak_core(n).wait_recv()
            pplane[n, 0] = jnp.maximum(pcore[n, 0], pcore[n, 1])
            over_plane(peak_plane(n), start)

    def sum_plane(n):
        over_plane(plane_out(n), wait_recv)
        total = psum[n, chip]
        for i in range(1, PLANE):
            total = total + rplane[n, i]
        zbuf[n, zed] = total
        for i in range(1, DEPTH):
            z_out(n, i).start()
        if n < 2:
            over_plane(peak_plane(n), wait_recv)
            top = pplane[n, 0]
            for i in range(1, PLANE):
                top = jnp.maximum(top, pplane[n, i])
            pz[n, 0] = top
            for i in range(1, DEPTH):
                peak_z(n, i).start()

    def sum_z(n):
        h = n % 2
        lanes = slice(h * HALF, (h + 1) * HALF)
        for i in range(1, DEPTH):
            z_in(n, i).wait_recv()
        total = weight * (((zbuf[n, 0] + zbuf[n, 1]) + zbuf[n, 2]) + zbuf[n, 3])
        if n < 2:
            for i in range(1, DEPTH):
                peak_z(n, i).wait_recv()
            top = jnp.maximum(jnp.maximum(pz[n, 0], pz[n, 1]), jnp.maximum(pz[n, 2], pz[n, 3]))
            step = STEP_LIMIT / (1.0 + top)
            steps[h] = step
            rate_one[h] = total
            cbuf[2 + h, chip, core] = coeffs[:, lanes] + step * total
            over_plane(gather_out(2 + h), start)
        else:
            mean_rate = (rate_one[h] + total) * 0.5
            rate_out[:, lanes] = mean_rate
            adv_out[:, lanes] = coeffs[:, lanes] + steps[h] * mean_rate

    def gather_plane(g):
        over_plane(gather_in(g), wait_recv)
        share_out(g).start()

    def gather_done(g):
        share_in(g).wait_recv()

    gather_plane(0)
    gather_done(0)
    set_coeffs(0)
    for k in range(2):
        large[k].wait_recv()
        large[2 + k].wait_recv()
    for k, at in ((0, 0), (1, ROWS + 1)):
        for part in range(2):
            rows = slice(part * 128, (part + 1) * 128)
            high, low = halves(halo_rows[k, rows, :])
            bt[at * COLS + part * 128:at * COLS + (part + 1) * 128, 0:MODES] = high
            bt[at * COLS + part * 128:at * COLS + (part + 1) * 128, MODES:2 * MODES] = low
        high, low = halves(halo_cols[k].reshape(ROWS, MODES))
        bt[EXT + 16 * k:EXT + 16 * (k + 1), 0:MODES] = high
        bt[EXT + 16 * k:EXT + 16 * (k + 1), MODES:2 * MODES] = low

    section_of(0, 0, ((7, lambda: gather_plane(1)),))
    sum_start(0)
    gather_done(1)
    set_coeffs(1)
    section_of(0, 1, ((3, lambda: sum_core(0)), (11, lambda: sum_plane(0))))
    sum_start(1)
    sum_z(0)
    sum_core(1)
    gather_plane(2)
    sum_plane(1)
    gather_done(2)
    set_coeffs(2)
    section_of(1, 0, ((2, lambda: sum_z(1)), (9, lambda: gather_plane(3))))
    sum_start(2)
    gather_done(3)
    set_coeffs(3)
    section_of(1, 1, ((3, lambda: sum_core(2)), (11, lambda: sum_plane(2))))
    sum_start(3)
    sum_z(2)
    sum_core(3)
    sum_plane(3)
    sum_z(3)

    for c in small + large:
        c.wait_send()
    for g in range(4):
        over_plane(gather_out(g), wait_send)
        share_out(g).wait_send()
        core_out(g).wait_send()
        over_plane(plane_out(g), wait_send)
        for i in range(1, DEPTH):
            z_out(g, i).wait_send()
    for h in range(2):
        peak_core(h).wait_send()
        over_plane(peak_plane(h), wait_send)
        for i in range(1, DEPTH):
            peak_z(h, i).wait_send()


def per_device(weight, coeffs, pod_basis, mean_field, velocity, diffusivity, reaction):
    flat = pod_basis.reshape(MODES * ROWS, COLS)
    vmem = lambda *shape: pltpu.VMEM(shape, F32)
    narrow = lambda *shape: pltpu.VMEM(shape, BF16)
    dma = lambda *shape: pltpu.SemaphoreType.DMA(shape)
    whole = pl.BlockSpec(memory_space=pltpu.VMEM)
    scratch = [
        vmem(2, MODES * ROWS, 128),
        narrow(EXT + 32, 2 * MODES),
        narrow(ROWS, MODES, 2 * COLS),
        vmem(6, ROWS, COLS, 128),
        vmem(EXT + 32, 128),
        vmem(2, ROWS + 2, ROWPAD, 128),
        narrow(2, COLS, HALF),
        narrow(2, COLS, HALF),
        narrow(MODES, HALF),
        narrow(MODES, HALF),
        vmem(4, PLANE, 2, 16, HALF),
        vmem(4, PLANE, 16, HALF),
        vmem(4, PLANE, 16, HALF),
        vmem(4, PLANE, 16, HALF),
        vmem(4, DEPTH, 16, HALF),
        vmem(4, PLANE, 2, 16, HALF),
        vmem(2, 16, HALF),
        vmem(2, 1, HALF),
        vmem(2, COLS, MODES),
        vmem(2, COLS, MODES),
        vmem(2, ROWS, 1, MODES),
        vmem(2, ROWS, 1, MODES),
        vmem(2, 8, COLS),
        vmem(2, 8, COLS),
        vmem(2, ROWS, 128),
        vmem(2, ROWS, 128),
        vmem(ROWS + 2, 8, COLS),
        vmem(2, 8, HALF),
        vmem(2, 2, 1, HALF),
        vmem(2, PLANE, 1, HALF),
        vmem(2, DEPTH, 1, HALF),
        dma(2),
        dma(4, PLANE), dma(4, PLANE), dma(4), dma(4),
        dma(3, 4), dma(3, 4), dma(4), dma(4),
        dma(4, PLANE), dma(4, PLANE), dma(4, DEPTH), dma(4, DEPTH),
        dma(2), dma(2), dma(2, PLANE), dma(2, PLANE), dma(2, DEPTH), dma(2, DEPTH),
    ]
    out = jax.ShapeDtypeStruct((16, TRAJ), F32)
    return pl.pallas_call(
        functools.partial(kernel, weight),
        out_shape=(out, out),
        in_specs=[whole, pl.BlockSpec(memory_space=pl.ANY), whole, whole, whole, whole],
        out_specs=(whole, whole),
        scratch_shapes=scratch,
        compiler_params=pltpu.CompilerParams(
            collective_id=0, has_side_effects=True, vmem_limit_bytes=67043328
        ),
    )(coeffs, flat, mean_field, velocity, diffusivity, reaction)


def solution(mesh):
    cells = ROWS * COLS * mesh.shape["wide"] * mesh.shape["col"]
    weight = math.sqrt(MODES / cells)
    placed = (
        P("wide", None),
        P(None, "wide", "col"),
        P("wide", "col"),
        P(None, "wide", "col"),
        P("wide", "col"),
        P("wide", "col"),
    )
    return jax.shard_map(
        functools.partial(per_device, weight),
        mesh=mesh,
        in_specs=placed,
        out_specs=(P("wide", None), P("wide", None)),
        check_vma=False,
    )
```

```python
import functools
import math

import jax
import jax.numpy as jnp
from jax import lax
from jax.experimental import pallas as pl
from jax.experimental.pallas import tpu as pltpu
from jax.sharding import PartitionSpec as P

MODES = 512
TRAJ = 512
ROWS = 16
COLS = 256
HALF = 256
PLANE = 16
DEPTH = 4
MESH = pl.DeviceIdType.MESH
F32 = jnp.float32
BF16 = jnp.bfloat16
STEP_LIMIT = 2.0
PAD = 8
ROWPAD = COLS + 2 * PAD
CELLS = ROWS * COLS
EXT = (ROWS + 2) * COLS


def halves(value):
    high = value.astype(BF16)
    return high, (value - high.astype(F32)).astype(BF16)


def kernel(
    weight,
    coeffs, basis, mean, vel, diff, reac,
    adv_out, rate_out,
    stage, bt, bn, kx, ab, mb, field, shi_a, shi_b, slo_a, slo_b, chi, clo,
    pacc, psum, rcore, rplane, zbuf, cbuf, rate_one, steps,
    edge_rows, halo_rows, edge_cols, halo_cols,
    vrow, mrow, vcol, mcol, kc,
    peak, pcore, pplane, pz,
    load_sem, ag_send, ag_recv, agc_send, agc_recv,
    hal_send, hal_recv, core_send, core_recv, pl_send, pl_recv, z_send, z_recv,
    pkc_send, pkc_recv, pkp_send, pkp_recv, pkz_send, pkz_recv,
):
    wide = lax.axis_index("wide")
    zed = lax.axis_index("col")
    chip = wide // 2
    core = wide % 2
    partner = wide + 1 - 2 * core
    down = (wide + 1) % (2 * PLANE)
    up = (wide + 2 * PLANE - 1) % (2 * PLANE)
    beside = (wide + 2 * PLANE + 2 * core - 1) % (2 * PLANE)

    def plane_peer(i):
        return 2 * ((chip + i) % PLANE) + core

    def load_copy(x):
        return pltpu.make_async_copy(basis.at[:, x, :], stage.at[x], load_sem.at[x])

    load_copy(ROWS - 1).start()
    for x in range(ROWS - 1):
        load_copy(x).start()

    barrier = pltpu.get_barrier_semaphore()

    def signal(to_wide, to_zed):
        pl.semaphore_signal(barrier, inc=1, device_id=(to_wide, to_zed), device_id_type=MESH)

    signal(partner, zed)
    signal(beside, zed)

    def greet_plane(i, carry):
        signal(plane_peer(i), zed)
        return carry

    lax.fori_loop(1, PLANE, greet_plane, 0)
    for i in range(1, DEPTH):
        signal(wide, (zed + i) % DEPTH)
    pl.semaphore_wait(barrier, 2 + PLANE - 1 + DEPTH - 1)

    def remote(src, dst, send, recv, to_wide, to_zed):
        return pltpu.make_async_remote_copy(
            src_ref=src, dst_ref=dst, send_sem=send, recv_sem=recv,
            device_id=(to_wide, to_zed), device_id_type=MESH,
        )

    def over_plane(make, act):
        def body(i, carry):
            act(make(i))
            return carry

        lax.fori_loop(1, PLANE, body, 0)

    start = lambda c: c.start()
    wait_recv = lambda c: c.wait_recv()
    wait_send = lambda c: c.wait_send()

    def gather_out(g):
        def make(i):
            own = cbuf.at[g, chip, core]
            return remote(own, own, ag_send.at[g, i], ag_recv.at[g, i], plane_peer(i), zed)

        return make

    def gather_in(g):
        def make(i):
            slot = cbuf.at[g, (chip + PLANE - i) % PLANE, core]
            return remote(slot, slot, ag_send.at[g, i], ag_recv.at[g, i], plane_peer(i), zed)

        return make

    def share_out(g):
        mine = cbuf.at[g, :, core]
        return remote(mine, mine, agc_send.at[g], agc_recv.at[g], partner, zed)

    def share_in(g):
        theirs = cbuf.at[g, :, 1 - core]
        return remote(theirs, theirs, agc_send.at[g], agc_recv.at[g], partner, zed)

    left = (zed + DEPTH - 1) % DEPTH
    right = (zed + 1) % DEPTH
    small = []
    for k, (to_wide, to_zed) in enumerate(((down, zed), (up, zed), (wide, right), (wide, left))):
        if k < 2:
            part = pl.ds(8 * (1 - k), 8)
            small.append(remote(vel.at[0, part, :], vrow.at[k], hal_send.at[0, k], hal_recv.at[0, k], to_wide, to_zed))
            small.append(remote(mean.at[part, :], mrow.at[k], hal_send.at[1, k], hal_recv.at[1, k], to_wide, to_zed))
        else:
            part = pl.ds(128 * (3 - k), 128)
            small.append(remote(vel.at[1, :, part], vcol.at[k - 2], hal_send.at[0, k], hal_recv.at[0, k], to_wide, to_zed))
            small.append(remote(mean.at[:, part], mcol.at[k - 2], hal_send.at[1, k], hal_recv.at[1, k], to_wide, to_zed))
    large = [
        remote(edge_rows.at[0], halo_rows.at[0], hal_send.at[2, 0], hal_recv.at[2, 0], down, zed),
        remote(edge_rows.at[1], halo_rows.at[1], hal_send.at[2, 1], hal_recv.at[2, 1], up, zed),
        remote(edge_cols.at[0], halo_cols.at[0], hal_send.at[2, 2], hal_recv.at[2, 2], wide, right),
        remote(edge_cols.at[1], halo_cols.at[1], hal_send.at[2, 3], hal_recv.at[2, 3], wide, left),
    ]

    for g in range(2):
        cbuf[g, chip, core] = coeffs[:, g * HALF:(g + 1) * HALF]
    over_plane(gather_out(0), start)
    for c in small:
        c.start()
    over_plane(gather_out(1), start)

    unit = (
        lax.broadcasted_iota(jnp.int32, (COLS, COLS), 0) == lax.broadcasted_iota(jnp.int32, (COLS, COLS), 1)
    ).astype(BF16)

    def prepare(x, edge):
        load_copy(x).wait()
        high, low = halves(stage[x])
        bn[x, :, 0:COLS] = high
        bn[x, :, COLS:2 * COLS] = low
        turn = lambda part: lax.dot_general(unit, part, (((1,), (1,)), ((), ())), preferred_element_type=F32)
        high = turn(high)
        low = turn(low)
        at = pl.ds(pl.multiple_of((x + 1) * COLS, COLS), COLS)
        bt[at, 0:MODES] = high.astype(BF16)
        bt[at, MODES:2 * MODES] = low.astype(BF16)
        if edge is not None:
            edge_rows[edge] = high + low
        edge_cols[0, x] = high[COLS - 1:COLS] + low[COLS - 1:COLS]
        edge_cols[1, x] = high[0:1] + low[0:1]

    prepare(ROWS - 1, 0)
    large[0].start()
    prepare(0, 1)
    large[1].start()

    def prepare_inner(x, carry):
        prepare(x, None)
        return carry

    lax.fori_loop(1, ROWS - 1, prepare_inner, 0)
    large[2].start()
    large[3].start()

    def spread(cells, k):
        return jnp.broadcast_to(cells[:, k:k + 1], (cells.shape[0], 128))

    for c in small:
        c.wait_recv()
    vx = vel[0]
    vy = vel[1]
    row_id = lax.broadcasted_iota(jnp.int32, (ROWS, COLS), 0)
    col_id = lax.broadcasted_iota(jnp.int32, (ROWS, COLS), 1)
    vx_next = jnp.where(row_id == ROWS - 1, jnp.broadcast_to(vrow[1, 0:1, :], (ROWS, COLS)), pltpu.roll(vx, ROWS - 1, 0))
    vx_prev = jnp.where(row_id == 0, jnp.broadcast_to(vrow[0, 7:8, :], (ROWS, COLS)), pltpu.roll(vx, 1, 0))
    vy_next = jnp.where(col_id == COLS - 1, jnp.broadcast_to(vcol[1, :, 0:1], (ROWS, COLS)), pltpu.roll(vy, COLS - 1, 1))
    vy_prev = jnp.where(col_id == 0, jnp.broadcast_to(vcol[0, :, 127:128], (ROWS, COLS)), pltpu.roll(vy, 1, 1))
    d = diff[...]
    zero_row = jnp.zeros((ROWS, COLS), F32)
    planes = (d - 0.5 * vx_next, d + 0.5 * vx_prev, d - 0.5 * vy_next, d + 0.5 * vy_prev, -4.0 * d, reac[...], mean[...], zero_row)
    for k, values in enumerate(planes):
        kc[0:ROWS, k, :] = values
        kc[ROWS:2 * ROWS, k, :] = zero_row
    kc[ROWS] = jnp.broadcast_to(mrow[0, 7:8, :], (8, COLS))
    kc[ROWS + 1] = jnp.broadcast_to(mrow[1, 0:1, :], (8, COLS))
    turned = kc[...].reshape(COLS, COLS).T
    for x in range(ROWS):
        tile = turned[:, 0:128]
        kx[x] = tile if x == 0 else pltpu.roll(tile, 128 - 8 * x, 1)
    mb[0:COLS, :] = spread(turned, 128)
    mb[EXT - COLS:EXT, :] = spread(turned, 136)
    mb[EXT:EXT + 16, :] = jnp.broadcast_to(mcol[0, :, 127:128], (16, 128))
    mb[EXT + 16:EXT + 32, :] = jnp.broadcast_to(mcol[1, :, 0:1], (16, 128))

    def spread_row(x, carry):
        cells = kx[x]
        for k in range(6):
            ab[k, x] = spread(cells, k)
        mb[pl.ds(pl.multiple_of((x + 1) * COLS, COLS), COLS), :] = spread(cells, 6)
        return carry

    lax.fori_loop(0, ROWS, spread_row, 0)

    shi = (shi_a, shi_b)
    slo = (slo_a, slo_b)

    def set_coeffs(g):
        high, low = halves(cbuf[g].reshape(MODES, HALF))
        chi[...] = high
        clo[...] = low

    def expand_rows(at, count):
        rows = bt[pl.ds(at, count), :]
        left_side = jnp.concatenate([rows, rows[:, 0:MODES]], axis=1)
        ch = chi[...]
        right_side = jnp.concatenate([ch, ch, clo[...]], axis=0)
        total = jnp.dot(left_side, right_side, preferred_element_type=F32)
        centre = mb[pl.ds(at, count), :]
        return [total[:, lt * 128:(lt + 1) * 128] + centre for lt in range(2)]

    def expand(i):
        at = pl.multiple_of(i * COLS, COLS)
        for lt, values in enumerate(expand_rows(at, COLS)):
            field[lt, i, PAD:PAD + COLS, :] = values

    def expand_sides():
        for lt, values in enumerate(expand_rows(EXT, 32)):
            for x in range(ROWS):
                field[lt, x + 1, PAD - 1:PAD, :] = values[x:x + 1]
                field[lt, x + 1, PAD + COLS:PAD + COLS + 1, :] = values[16 + x:17 + x]

    def source(r, slot, section, h):
        i = r + 1
        for lt in range(2):
            lanes = slice(lt * 128, (lt + 1) * 128)
            here = field[lt, i, PAD:PAD + COLS, :]
            total = ab[0, r] * field[lt, i + 1, PAD:PAD + COLS, :]
            total += ab[1, r] * field[lt, i - 1, PAD:PAD + COLS, :]
            total += ab[2, r] * field[lt, i, PAD + 1:PAD + COLS + 1, :]
            total += ab[3, r] * field[lt, i, PAD - 1:PAD + COLS - 1, :]
            total += ab[4, r] * here
            total += ab[5, r] * jnp.tanh(here)
            high, low = halves(total)
            shi[slot][:, lanes] = high
            slo[slot][:, lanes] = low
            if section == 0:
                tops = jnp.max(jnp.abs(here).reshape(COLS // 8, 8, 128), axis=0)
                peak[h, :, lanes] = jnp.maximum(peak[h, :, lanes], tops)

    def project(r, slot, n):
        sides = bn[r]
        left_side = jnp.concatenate([sides, sides[:, 0:COLS]], axis=1)
        sh = shi[slot][...]
        right_side = jnp.concatenate([sh, sh, slo[slot][...]], axis=0)
        part = jnp.dot(left_side, right_side, preferred_element_type=F32)
        pacc[n] = pacc[n] + part.reshape(PLANE, 2, 16, HALF)

    def section_of(section, h, hooks):
        n = 2 * section + h
        expand_sides()
        for i in range(3):
            expand(i)
        pacc[n] = jnp.zeros((PLANE, 2, 16, HALF), F32)
        if section == 0:
            peak[h] = jnp.zeros((8, HALF), F32)
        expand(3)
        source(0, 0, section, h)

        def body(r, carry):
            for at, hook in hooks:
                pl.when(r == at // 2)(hook)
            for k in range(2):
                project(2 * r + k, k, n)
                source(2 * r + 1 + k, 1 - k, section, h)
                expand(2 * r + 4 + k)
            return carry

        lax.fori_loop(0, ROWS // 2 - 1, body, 0)
        project(ROWS - 2, 0, n)
        source(ROWS - 1, 1, section, h)
        project(ROWS - 1, 1, n)

    def core_out(n):
        return remote(pacc.at[n, :, 1 - core], rcore.at[n], core_send.at[n], core_recv.at[n], partner, zed)

    def peak_core(h):
        return remote(pcore.at[h, 0], pcore.at[h, 1], pkc_send.at[h], pkc_recv.at[h], partner, zed)

    def plane_out(n):
        def make(i):
            return remote(
                psum.at[n, (chip + i) % PLANE], rplane.at[n, i], pl_send.at[n, i], pl_recv.at[n, i], plane_peer(i), zed
            )

        return make

    def peak_plane(h):
        def make(i):
            return remote(pplane.at[h, 0], pplane.at[h, i], pkp_send.at[h, i], pkp_recv.at[h, i], plane_peer(i), zed)

        return make

    def z_out(n, i):
        mine = zbuf.at[n, zed]
        return remote(mine, mine, z_send.at[n, i], z_recv.at[n, i], wide, (zed + i) % DEPTH)

    def z_in(n, i):
        slot = zbuf.at[n, (zed + DEPTH - i) % DEPTH]
        return remote(slot, slot, z_send.at[n, i], z_recv.at[n, i], wide, (zed + i) % DEPTH)

    def peak_z(h, i):
        return remote(pz.at[h, 0], pz.at[h, i], pkz_send.at[h, i], pkz_recv.at[h, i], wide, (zed + i) % DEPTH)

    def sum_start(n):
        core_out(n).start()
        if n < 2:
            pcore[n, 0] = jnp.max(peak[n], axis=0, keepdims=True)
            peak_core(n).start()

    def sum_core(n):
        core_out(n).wait_recv()
        psum[n] = pacc[n, :, core] + rcore[n]
        over_plane(plane_out(n), start)
        if n < 2:
            peak_core(n).wait_recv()
            pplane[n, 0] = jnp.maximum(pcore[n, 0], pcore[n, 1])
            over_plane(peak_plane(n), start)

    def sum_plane(n):
        over_plane(plane_out(n), wait_recv)
        total = psum[n, chip]
        for i in range(1, PLANE):
            total = total + rplane[n, i]
        zbuf[n, zed] = total
        for i in range(1, DEPTH):
            z_out(n, i).start()
        if n < 2:
            over_plane(peak_plane(n), wait_recv)
            top = pplane[n, 0]
            for i in range(1, PLANE):
                top = jnp.maximum(top, pplane[n, i])
            pz[n, 0] = top
            for i in range(1, DEPTH):
                peak_z(n, i).start()

    def sum_z(n):
        h = n % 2
        lanes = slice(h * HALF, (h + 1) * HALF)
        for i in range(1, DEPTH):
            z_in(n, i).wait_recv()
        total = weight * (((zbuf[n, 0] + zbuf[n, 1]) + zbuf[n, 2]) + zbuf[n, 3])
        if n < 2:
            for i in range(1, DEPTH):
                peak_z(n, i).wait_recv()
            top = jnp.maximum(jnp.maximum(pz[n, 0], pz[n, 1]), jnp.maximum(pz[n, 2], pz[n, 3]))
            step = STEP_LIMIT / (1.0 + top)
            steps[h] = step
            rate_one[h] = total
            cbuf[2 + h, chip, core] = coeffs[:, lanes] + step * total
            over_plane(gather_out(2 + h), start)
        else:
            mean_rate = (rate_one[h] + total) * 0.5
            rate_out[:, lanes] = mean_rate
            adv_out[:, lanes] = coeffs[:, lanes] + steps[h] * mean_rate

    def gather_plane(g):
        over_plane(gather_in(g), wait_recv)
        share_out(g).start()

    def gather_done(g):
        share_in(g).wait_recv()

    gather_plane(0)
    gather_done(0)
    set_coeffs(0)
    for k in range(2):
        large[k].wait_recv()
        large[2 + k].wait_recv()
    for k, at in ((0, 0), (1, ROWS + 1)):
        for part in range(2):
            rows = slice(part * 128, (part + 1) * 128)
            high, low = halves(halo_rows[k, rows, :])
            bt[at * COLS + part * 128:at * COLS + (part + 1) * 128, 0:MODES] = high
            bt[at * COLS + part * 128:at * COLS + (part + 1) * 128, MODES:2 * MODES] = low
        high, low = halves(halo_cols[k].reshape(ROWS, MODES))
        bt[EXT + 16 * k:EXT + 16 * (k + 1), 0:MODES] = high
        bt[EXT + 16 * k:EXT + 16 * (k + 1), MODES:2 * MODES] = low

    section_of(0, 0, ((7, lambda: gather_plane(1)),))
    sum_start(0)
    gather_done(1)
    set_coeffs(1)
    section_of(0, 1, ((3, lambda: sum_core(0)), (11, lambda: sum_plane(0))))
    sum_start(1)
    sum_z(0)
    sum_core(1)
    gather_plane(2)
    sum_plane(1)
    gather_done(2)
    set_coeffs(2)
    section_of(1, 0, ((2, lambda: sum_z(1)), (9, lambda: gather_plane(3))))
    sum_start(2)
    gather_done(3)
    set_coeffs(3)
    section_of(1, 1, ((3, lambda: sum_core(2)), (11, lambda: sum_plane(2))))
    sum_start(3)
    sum_z(2)
    sum_core(3)
    sum_plane(3)
    sum_z(3)

    for c in small + large:
        c.wait_send()
    for g in range(4):
        over_plane(gather_out(g), wait_send)
        share_out(g).wait_send()
        core_out(g).wait_send()
        over_plane(plane_out(g), wait_send)
        for i in range(1, DEPTH):
            z_out(g, i).wait_send()
    for h in range(2):
        peak_core(h).wait_send()
        over_plane(peak_plane(h), wait_send)
        for i in range(1, DEPTH):
            peak_z(h, i).wait_send()


def per_device(weight, coeffs, pod_basis, mean_field, velocity, diffusivity, reaction):
    vmem = lambda *shape: pltpu.VMEM(shape, F32)
    narrow = lambda *shape: pltpu.VMEM(shape, BF16)
    dma = lambda *shape: pltpu.SemaphoreType.DMA(shape)
    whole = pl.BlockSpec(memory_space=pltpu.VMEM)
    scratch = [
        vmem(ROWS, MODES, COLS),
        narrow(EXT + 32, 2 * MODES),
        narrow(ROWS, MODES, 2 * COLS),
        vmem(ROWS, COLS, 128),
        vmem(6, ROWS, COLS, 128),
        vmem(EXT + 32, 128),
        vmem(2, ROWS + 2, ROWPAD, 128),
        narrow(COLS, HALF),
        narrow(COLS, HALF),
        narrow(COLS, HALF),
        narrow(COLS, HALF),
        narrow(MODES, HALF),
        narrow(MODES, HALF),
        vmem(4, PLANE, 2, 16, HALF),
        vmem(4, PLANE, 16, HALF),
        vmem(4, PLANE, 16, HALF),
        vmem(4, PLANE, 16, HALF),
        vmem(4, DEPTH, 16, HALF),
        vmem(4, PLANE, 2, 16, HALF),
        vmem(2, 16, HALF),
        vmem(2, 1, HALF),
        vmem(2, COLS, MODES),
        vmem(2, COLS, MODES),
        vmem(2, ROWS, 1, MODES),
        vmem(2, ROWS, 1, MODES),
        vmem(2, 8, COLS),
        vmem(2, 8, COLS),
        vmem(2, ROWS, 128),
        vmem(2, ROWS, 128),
        vmem(2 * ROWS, 8, COLS),
        vmem(2, 8, HALF),
        vmem(2, 2, 1, HALF),
        vmem(2, PLANE, 1, HALF),
        vmem(2, DEPTH, 1, HALF),
        dma(ROWS),
        dma(4, PLANE), dma(4, PLANE), dma(4), dma(4),
        dma(3, 4), dma(3, 4), dma(4), dma(4),
        dma(4, PLANE), dma(4, PLANE), dma(4, DEPTH), dma(4, DEPTH),
        dma(2), dma(2), dma(2, PLANE), dma(2, PLANE), dma(2, DEPTH), dma(2, DEPTH),
    ]
    out = jax.ShapeDtypeStruct((16, TRAJ), F32)
    return pl.pallas_call(
        functools.partial(kernel, weight),
        out_shape=(out, out),
        in_specs=[whole, pl.BlockSpec(memory_space=pl.ANY), whole, whole, whole, whole],
        out_specs=(whole, whole),
        scratch_shapes=scratch,
        compiler_params=pltpu.CompilerParams(
            collective_id=0, has_side_effects=True, vmem_limit_bytes=67043328
        ),
    )(coeffs, pod_basis, mean_field, velocity, diffusivity, reaction)


def solution(mesh):
    cells = ROWS * COLS * mesh.shape["wide"] * mesh.shape["col"]
    weight = math.sqrt(MODES / cells)
    placed = (
        P("wide", None),
        P(None, "wide", "col"),
        P("wide", "col"),
        P(None, "wide", "col"),
        P("wide", "col"),
        P("wide", "col"),
    )
    return jax.shard_map(
        functools.partial(per_device, weight),
        mesh=mesh,
        in_specs=placed,
        out_specs=(P("wide", None), P("wide", None)),
        check_vma=False,
    )
```

```python
import functools
import math

import jax
import jax.numpy as jnp
from jax import lax
from jax.experimental import pallas as pl
from jax.experimental.pallas import tpu as pltpu
from jax.sharding import PartitionSpec as P

MODES = 512
TRAJ = 512
ROWS = 16
COLS = 256
HALF = 256
PLANE = 16
DEPTH = 4
MESH = pl.DeviceIdType.MESH
F32 = jnp.float32
BF16 = jnp.bfloat16
STEP_LIMIT = 2.0
PAD = 8
ROWPAD = COLS + 2 * PAD
CELLS = ROWS * COLS
EXT = (ROWS + 2) * COLS


def halves(value):
    high = value.astype(BF16)
    return high, (value - high.astype(F32)).astype(BF16)


def kernel(
    weight,
    coeffs, basis, mean, vel, diff, reac,
    adv_out, rate_out,
    stage, bt, bn, kx, ab, mb, field, shi_a, shi_b, slo_a, slo_b, chi, clo,
    pacc, psum, rcore, rplane, zbuf, cbuf, rate_one, steps,
    edge_rows, halo_rows, edge_cols, halo_cols,
    vrow, mrow, vcol, mcol, kc,
    peak, pcore, pplane, pz,
    load_sem, ag_send, ag_recv, agc_send, agc_recv,
    hal_send, hal_recv, core_send, core_recv, pl_send, pl_recv, z_send, z_recv,
    pkc_send, pkc_recv, pkp_send, pkp_recv, pkz_send, pkz_recv,
):
    wide = lax.axis_index("wide")
    zed = lax.axis_index("col")
    chip = wide // 2
    core = wide % 2
    partner = wide + 1 - 2 * core
    down = (wide + 1) % (2 * PLANE)
    up = (wide + 2 * PLANE - 1) % (2 * PLANE)
    beside = (wide + 2 * PLANE + 2 * core - 1) % (2 * PLANE)

    def plane_peer(i):
        return 2 * ((chip + i) % PLANE) + core

    def load_copy(x):
        return pltpu.make_async_copy(basis.at[:, x, :], stage.at[x], load_sem.at[x // 4])

    def loaded(group):
        part = stage.at[pl.ds(4 * group, 4)]
        pltpu.make_async_copy(part, part, load_sem.at[group]).wait()

    for x in (*range(12, 16), *range(12)):
        load_copy(x).start()

    barrier = pltpu.get_barrier_semaphore()

    def signal(to_wide, to_zed):
        pl.semaphore_signal(barrier, inc=1, device_id=(to_wide, to_zed), device_id_type=MESH)

    signal(partner, zed)
    signal(beside, zed)

    def greet_plane(i, carry):
        signal(plane_peer(i), zed)
        return carry

    lax.fori_loop(1, PLANE, greet_plane, 0)
    for i in range(1, DEPTH):
        signal(wide, (zed + i) % DEPTH)

    def remote(src, dst, send, recv, to_wide, to_zed):
        return pltpu.make_async_remote_copy(
            src_ref=src, dst_ref=dst, send_sem=send, recv_sem=recv,
            device_id=(to_wide, to_zed), device_id_type=MESH,
        )

    def over_plane(make, act):
        def body(i, carry):
            act(make(i))
            return carry

        lax.fori_loop(1, PLANE, body, 0)

    start = lambda c: c.start()
    wait_recv = lambda c: c.wait_recv()
    wait_send = lambda c: c.wait_send()

    def gather_out(g):
        def make(i):
            own = cbuf.at[g, chip, core]
            return remote(own, own, ag_send.at[g], ag_recv.at[g], plane_peer(i), zed)

        return make

    def gather_all(g):
        others = cbuf.at[g, 1:PLANE, 0]
        return remote(others, others, ag_send.at[g], ag_recv.at[g], partner, zed)

    def share(g, side):
        part = cbuf.at[g, :, side]
        return remote(part, part, agc_send.at[g], agc_recv.at[g], partner, zed)

    def gather_start(g):
        over_plane(gather_out(g), start)

    def gather_plane(g):
        gather_all(g).wait_recv()
        share(g, core).start()

    def gather_done(g):
        share(g, 1 - core).wait_recv()

    left = (zed + DEPTH - 1) % DEPTH
    right = (zed + 1) % DEPTH
    halos = (
        (vrow, vel.at[0, 8:16, :], vel.at[0, 0:8, :], 0),
        (mrow, mean.at[8:16, :], mean.at[0:8, :], 0),
        (vcol, vel.at[1, :, 128:256], vel.at[1, :, 0:128], 1),
        (mcol, mean.at[:, 128:256], mean.at[:, 0:128], 1),
        (halo_rows, edge_rows.at[0], edge_rows.at[1], 0),
        (halo_cols, edge_cols.at[0], edge_cols.at[1], 1),
    )

    def halo_start(k):
        held, first, second, sideways = halos[k]
        ahead, behind = ((wide, right), (wide, left)) if sideways else ((down, zed), (up, zed))
        remote(first, held.at[0], hal_send.at[k], hal_recv.at[k], *ahead).start()
        remote(second, held.at[1], hal_send.at[k], hal_recv.at[k], *behind).start()

    def halo_all(k):
        held = halos[k][0]
        return remote(held, held, hal_send.at[k], hal_recv.at[k], partner, zed)

    for g in range(2):
        cbuf[g, chip, core] = coeffs[:, g * HALF:(g + 1) * HALF]
    pl.semaphore_wait(barrier, 2 + PLANE - 1 + DEPTH - 1)
    gather_start(0)
    for k in range(4):
        halo_start(k)

    unit = (
        lax.broadcasted_iota(jnp.int32, (COLS, COLS), 0) == lax.broadcasted_iota(jnp.int32, (COLS, COLS), 1)
    ).astype(BF16)

    def prepare(x, edge):
        high, low = halves(stage[x])
        bn[x, :, 0:COLS] = high
        bn[x, :, COLS:2 * COLS] = low
        turn = lambda part: lax.dot_general(unit, part, (((1,), (1,)), ((), ())), preferred_element_type=F32)
        high = turn(high)
        low = turn(low)
        at = pl.ds(pl.multiple_of((x + 1) * COLS, COLS), COLS)
        bt[at, 0:MODES] = high.astype(BF16)
        bt[at, MODES:2 * MODES] = low.astype(BF16)
        if edge is not None:
            edge_rows[edge] = high + low
        edge_cols[0, x] = high[COLS - 1:COLS] + low[COLS - 1:COLS]
        edge_cols[1, x] = high[0:1] + low[0:1]

    def prepare_inner(x, carry):
        prepare(x, None)
        return carry

    loaded(3)
    prepare(ROWS - 1, 0)
    lax.fori_loop(12, ROWS - 1, prepare_inner, 0)
    loaded(0)
    prepare(0, 1)
    loaded(1)
    loaded(2)
    lax.fori_loop(1, 12, prepare_inner, 0)
    halo_start(5)
    gather_plane(0)
    halo_start(4)
    gather_start(1)

    def spread(cells, k):
        return jnp.broadcast_to(cells[:, k:k + 1], (cells.shape[0], 128))

    for k in range(4):
        halo_all(k).wait_recv()
    vx = vel[0]
    vy = vel[1]
    row_id = lax.broadcasted_iota(jnp.int32, (ROWS, COLS), 0)
    col_id = lax.broadcasted_iota(jnp.int32, (ROWS, COLS), 1)
    vx_next = jnp.where(row_id == ROWS - 1, jnp.broadcast_to(vrow[1, 0:1, :], (ROWS, COLS)), pltpu.roll(vx, ROWS - 1, 0))
    vx_prev = jnp.where(row_id == 0, jnp.broadcast_to(vrow[0, 7:8, :], (ROWS, COLS)), pltpu.roll(vx, 1, 0))
    vy_next = jnp.where(col_id == COLS - 1, jnp.broadcast_to(vcol[1, :, 0:1], (ROWS, COLS)), pltpu.roll(vy, COLS - 1, 1))
    vy_prev = jnp.where(col_id == 0, jnp.broadcast_to(vcol[0, :, 127:128], (ROWS, COLS)), pltpu.roll(vy, 1, 1))
    d = diff[...]
    zero_row = jnp.zeros((ROWS, COLS), F32)
    planes = (d - 0.5 * vx_next, d + 0.5 * vx_prev, d - 0.5 * vy_next, d + 0.5 * vy_prev, -4.0 * d, reac[...], mean[...], zero_row)
    for k, values in enumerate(planes):
        kc[0:ROWS, k, :] = values
        kc[ROWS:2 * ROWS, k, :] = zero_row
    kc[ROWS] = jnp.broadcast_to(mrow[0, 7:8, :], (8, COLS))
    kc[ROWS + 1] = jnp.broadcast_to(mrow[1, 0:1, :], (8, COLS))
    turned = kc[...].reshape(COLS, COLS).T
    for x in range(ROWS):
        tile = turned[:, 0:128]
        kx[x] = tile if x == 0 else pltpu.roll(tile, 128 - 8 * x, 1)
    mb[0:COLS, :] = spread(turned, 128)
    mb[EXT - COLS:EXT, :] = spread(turned, 136)
    mb[EXT:EXT + 16, :] = jnp.broadcast_to(mcol[0, :, 127:128], (16, 128))
    mb[EXT + 16:EXT + 32, :] = jnp.broadcast_to(mcol[1, :, 0:1], (16, 128))

    def spread_mean(x, carry):
        mb[pl.ds(pl.multiple_of((x + 1) * COLS, COLS), COLS), :] = spread(kx[x], 6)
        return carry

    lax.fori_loop(0, ROWS, spread_mean, 0)

    def spread_row(x):
        cells = kx[x]
        for k in range(6):
            ab[k, x] = spread(cells, k)

    shi = (shi_a, shi_b)
    slo = (slo_a, slo_b)

    def set_coeffs(g):
        high, low = halves(cbuf[g].reshape(MODES, HALF))
        chi[...] = high
        clo[...] = low

    def expand_rows(at, count):
        rows = bt[pl.ds(at, count), :]
        left_side = jnp.concatenate([rows, rows[:, 0:MODES]], axis=1)
        ch = chi[...]
        right_side = jnp.concatenate([ch, ch, clo[...]], axis=0)
        total = jnp.dot(left_side, right_side, preferred_element_type=F32)
        centre = mb[pl.ds(at, count), :]
        return [total[:, lt * 128:(lt + 1) * 128] + centre for lt in range(2)]

    def expand(i):
        at = pl.multiple_of(i * COLS, COLS)
        for lt, values in enumerate(expand_rows(at, COLS)):
            field[lt, i, PAD:PAD + COLS, :] = values

    def expand_sides():
        for lt, values in enumerate(expand_rows(EXT, 32)):
            for x in range(ROWS):
                field[lt, x + 1, PAD - 1:PAD, :] = values[x:x + 1]
                field[lt, x + 1, PAD + COLS:PAD + COLS + 1, :] = values[16 + x:17 + x]

    def source(r, slot, section, h):
        i = r + 1
        for lt in range(2):
            lanes = slice(lt * 128, (lt + 1) * 128)
            here = field[lt, i, PAD:PAD + COLS, :]
            total = ab[0, r] * field[lt, i + 1, PAD:PAD + COLS, :]
            total += ab[1, r] * field[lt, i - 1, PAD:PAD + COLS, :]
            total += ab[2, r] * field[lt, i, PAD + 1:PAD + COLS + 1, :]
            total += ab[3, r] * field[lt, i, PAD - 1:PAD + COLS - 1, :]
            total += ab[4, r] * here
            total += ab[5, r] * jnp.tanh(here)
            high, low = halves(total)
            shi[slot][:, lanes] = high
            slo[slot][:, lanes] = low
            if section == 0:
                tops = jnp.max(jnp.abs(here).reshape(COLS // 8, 8, 128), axis=0)
                peak[h, :, lanes] = jnp.maximum(peak[h, :, lanes], tops)

    def project(r, slot, n):
        sides = bn[r]
        left_side = jnp.concatenate([sides, sides[:, 0:COLS]], axis=1)
        sh = shi[slot][...]
        right_side = jnp.concatenate([sh, sh, slo[slot][...]], axis=0)
        part = jnp.dot(left_side, right_side, preferred_element_type=F32)
        pacc[n] = pacc[n] + part.reshape(PLANE, 2, 16, HALF)

    def section_of(section, h, hooks, before_rims):
        n = 2 * section + h
        prime = spread_row if n == 0 else lambda x: None
        prime(1)
        expand_sides()
        for i in range(1, 5):
            expand(i)
        pacc[n] = jnp.zeros((PLANE, 2, 16, HALF), F32)
        if section == 0:
            peak[h] = jnp.zeros((8, HALF), F32)
        source(1, 1, section, h)
        prime(2)

        def body(r, carry):
            for at, hook in hooks:
                pl.when(r == at)(hook)
            for k in range(2):
                project(2 * r + 1 + k, 1 - k, n)
                source(2 * r + 2 + k, k, section, h)
                prime(2 * r + 3 + k)
                expand(2 * r + 5 + k)
            return carry

        lax.fori_loop(0, ROWS // 2 - 2, body, 0)
        before_rims()
        prime(0)
        project(ROWS - 3, 1, n)
        source(ROWS - 2, 0, section, h)
        expand(0)
        project(ROWS - 2, 0, n)
        source(0, 1, section, h)
        prime(ROWS - 1)
        expand(ROWS + 1)
        project(0, 1, n)
        source(ROWS - 1, 0, section, h)
        project(ROWS - 1, 0, n)

    def core_out(n):
        return remote(pacc.at[n, :, 1 - core], rcore.at[n], core_send.at[n], core_recv.at[n], partner, zed)

    def peak_core(h):
        return remote(pcore.at[h, 0], pcore.at[h, 1], pkc_send.at[h], pkc_recv.at[h], partner, zed)

    def plane_out(n):
        def make(i):
            return remote(
                psum.at[n, (chip + i) % PLANE], rplane.at[n, i], pl_send.at[n], pl_recv.at[n], plane_peer(i), zed
            )

        return make

    def plane_all(n):
        return remote(psum.at[n, 1:PLANE], rplane.at[n, 1:PLANE], pl_send.at[n], pl_recv.at[n], partner, zed)

    def peak_plane(h):
        def make(i):
            return remote(pplane.at[h, 0], pplane.at[h, i], pkp_send.at[h], pkp_recv.at[h], plane_peer(i), zed)

        return make

    def peak_plane_all(h):
        others = pplane.at[h, 1:PLANE]
        return remote(others, others, pkp_send.at[h], pkp_recv.at[h], partner, zed)

    def z_start(n):
        mine = zbuf.at[n, zed]
        for i in range(1, DEPTH):
            remote(mine, mine, z_send.at[n], z_recv.at[n], wide, (zed + i) % DEPTH).start()

    def z_all(n):
        others = zbuf.at[n, 1:DEPTH]
        return remote(others, others, z_send.at[n], z_recv.at[n], partner, zed)

    def peak_z_start(h):
        for i in range(1, DEPTH):
            remote(pz.at[h, 0], pz.at[h, i], pkz_send.at[h], pkz_recv.at[h], wide, (zed + i) % DEPTH).start()

    def peak_z_all(h):
        others = pz.at[h, 1:DEPTH]
        return remote(others, others, pkz_send.at[h], pkz_recv.at[h], partner, zed)

    def sum_start(n):
        core_out(n).start()
        if n < 2:
            pcore[n, 0] = jnp.max(peak[n], axis=0, keepdims=True)
            peak_core(n).start()

    def sum_core(n):
        core_out(n).wait_recv()
        psum[n] = pacc[n, :, core] + rcore[n]
        over_plane(plane_out(n), start)
        if n < 2:
            peak_core(n).wait_recv()
            pplane[n, 0] = jnp.maximum(pcore[n, 0], pcore[n, 1])
            over_plane(peak_plane(n), start)

    def sum_plane(n):
        plane_all(n).wait_recv()
        total = psum[n, chip]
        for i in range(1, PLANE):
            total = total + rplane[n, i]
        zbuf[n, zed] = total
        z_start(n)
        if n < 2:
            peak_plane_all(n).wait_recv()
            top = pplane[n, 0]
            for i in range(1, PLANE):
                top = jnp.maximum(top, pplane[n, i])
            pz[n, 0] = top
            peak_z_start(n)

    def sum_z(n):
        h = n % 2
        lanes = slice(h * HALF, (h + 1) * HALF)
        z_all(n).wait_recv()
        total = weight * (((zbuf[n, 0] + zbuf[n, 1]) + zbuf[n, 2]) + zbuf[n, 3])
        if n < 2:
            peak_z_all(n).wait_recv()
            top = jnp.maximum(jnp.maximum(pz[n, 0], pz[n, 1]), jnp.maximum(pz[n, 2], pz[n, 3]))
            step = STEP_LIMIT / (1.0 + top)
            steps[h] = step
            rate_one[h] = total
            cbuf[2 + h, chip, core] = coeffs[:, lanes] + step * total
            gather_start(2 + h)
        else:
            mean_rate = (rate_one[h] + total) * 0.5
            rate_out[:, lanes] = mean_rate
            adv_out[:, lanes] = coeffs[:, lanes] + steps[h] * mean_rate

    def split_into(values, at):
        high, low = halves(values)
        bt[at:at + values.shape[0], 0:MODES] = high
        bt[at:at + values.shape[0], MODES:2 * MODES] = low

    def rims():
        halo_all(4).wait_recv()
        for k, at in ((0, 0), (1, ROWS + 1)):
            for part in range(2):
                split_into(halo_rows[k, part * 128:(part + 1) * 128, :], at * COLS + part * 128)

    nothing = lambda: None
    halo_all(5).wait_recv()
    for k in range(2):
        split_into(halo_cols[k].reshape(ROWS, MODES), EXT + 16 * k)
    gather_done(0)
    set_coeffs(0)
    section_of(0, 0, ((5, lambda: gather_plane(1)),), rims)
    sum_start(0)
    gather_done(1)
    set_coeffs(1)
    section_of(0, 1, ((1, lambda: sum_core(0)), (5, lambda: sum_plane(0))), nothing)
    sum_start(1)
    sum_z(0)
    sum_core(1)
    gather_plane(2)
    sum_plane(1)
    gather_done(2)
    set_coeffs(2)
    section_of(1, 0, ((2, lambda: sum_z(1)), (5, lambda: gather_plane(3))), nothing)
    sum_start(2)
    gather_done(3)
    set_coeffs(3)
    section_of(1, 1, ((1, lambda: sum_core(2)), (5, lambda: sum_plane(2))), nothing)
    sum_start(3)
    sum_z(2)
    sum_core(3)
    sum_plane(3)
    sum_z(3)

    for k in range(6):
        halo_all(k).wait_send()
    for g in range(4):
        for sent in (gather_all(g), share(g, core), core_out(g), plane_all(g), z_all(g)):
            sent.wait_send()
    for h in range(2):
        for sent in (peak_core(h), peak_plane_all(h), peak_z_all(h)):
            sent.wait_send()


def per_device(weight, coeffs, pod_basis, mean_field, velocity, diffusivity, reaction):
    vmem = lambda *shape: pltpu.VMEM(shape, F32)
    narrow = lambda *shape: pltpu.VMEM(shape, BF16)
    dma = lambda *shape: pltpu.SemaphoreType.DMA(shape)
    whole = pl.BlockSpec(memory_space=pltpu.VMEM)
    scratch = [
        vmem(ROWS, MODES, COLS),
        narrow(EXT + 32, 2 * MODES),
        narrow(ROWS, MODES, 2 * COLS),
        vmem(ROWS, COLS, 128),
        vmem(6, ROWS, COLS, 128),
        vmem(EXT + 32, 128),
        vmem(2, ROWS + 2, ROWPAD, 128),
        narrow(COLS, HALF),
        narrow(COLS, HALF),
        narrow(COLS, HALF),
        narrow(COLS, HALF),
        narrow(MODES, HALF),
        narrow(MODES, HALF),
        vmem(4, PLANE, 2, 16, HALF),
        vmem(4, PLANE, 16, HALF),
        vmem(4, PLANE, 16, HALF),
        vmem(4, PLANE, 16, HALF),
        vmem(4, DEPTH, 16, HALF),
        vmem(4, PLANE, 2, 16, HALF),
        vmem(2, 16, HALF),
        vmem(2, 1, HALF),
        vmem(2, COLS, MODES),
        vmem(2, COLS, MODES),
        vmem(2, ROWS, 1, MODES),
        vmem(2, ROWS, 1, MODES),
        vmem(2, 8, COLS),
        vmem(2, 8, COLS),
        vmem(2, ROWS, 128),
        vmem(2, ROWS, 128),
        vmem(2 * ROWS, 8, COLS),
        vmem(2, 8, HALF),
        vmem(2, 2, 1, HALF),
        vmem(2, PLANE, 1, HALF),
        vmem(2, DEPTH, 1, HALF),
        dma(4),
        dma(4), dma(4), dma(4), dma(4),
        dma(6), dma(6), dma(4), dma(4),
        dma(4), dma(4), dma(4), dma(4),
        dma(2), dma(2), dma(2), dma(2), dma(2), dma(2),
    ]
    out = jax.ShapeDtypeStruct((16, TRAJ), F32)
    return pl.pallas_call(
        functools.partial(kernel, weight),
        out_shape=(out, out),
        in_specs=[whole, pl.BlockSpec(memory_space=pl.ANY), whole, whole, whole, whole],
        out_specs=(whole, whole),
        scratch_shapes=scratch,
        compiler_params=pltpu.CompilerParams(
            collective_id=0, has_side_effects=True, vmem_limit_bytes=67043328
        ),
    )(coeffs, pod_basis, mean_field, velocity, diffusivity, reaction)


def solution(mesh):
    cells = ROWS * COLS * mesh.shape["wide"] * mesh.shape["col"]
    weight = math.sqrt(MODES / cells)
    placed = (
        P("wide", None),
        P(None, "wide", "col"),
        P("wide", "col"),
        P(None, "wide", "col"),
        P("wide", "col"),
        P("wide", "col"),
    )
    return jax.shard_map(
        functools.partial(per_device, weight),
        mesh=mesh,
        in_specs=placed,
        out_specs=(P("wide", None), P("wide", None)),
        check_vma=False,
    )
```

```python
import functools
import math

import jax
import jax.numpy as jnp
from jax import lax
from jax.experimental import pallas as pl
from jax.experimental.pallas import tpu as pltpu
from jax.sharding import PartitionSpec as P

MODES = 512
TRAJ = 512
ROWS = 16
COLS = 256
HALF = 256
PLANE = 16
DEPTH = 4
MESH = pl.DeviceIdType.MESH
F32 = jnp.float32
BF16 = jnp.bfloat16
STEP_LIMIT = 2.0
PAD = 8
ROWPAD = COLS + 2 * PAD
CELLS = ROWS * COLS
EXT = (ROWS + 2) * COLS


def halves(value):
    high = value.astype(BF16)
    return high, (value - high.astype(F32)).astype(BF16)


def kernel(
    weight,
    given_coeffs, basis, given_mean, given_vel, given_diff, given_reac,
    rate_one, rate_two, step_out,
    coeffs, mean, vel, diff, reac, stage, bt, bn, kx, ab, mb, field, shi_a, shi_b, slo_a, slo_b, chi, clo,
    pacc, psum, rcore, rplane, zbuf, cbuf,
    edge_rows, halo_rows, edge_cols, halo_cols,
    vrow, mrow, vcol, mcol, kc,
    peak, pcore, pplane, pz,
    in_sem, load_sem, ag_send, ag_recv, agc_send, agc_recv,
    hal_send, hal_recv, core_send, core_recv, pl_send, pl_recv, z_send, z_recv,
    pkc_send, pkc_recv, pkp_send, pkp_recv, pkz_send, pkz_recv,
):
    wide = lax.axis_index("wide")
    zed = lax.axis_index("col")
    chip = wide // 2
    core = wide % 2
    partner = wide + 1 - 2 * core
    down = (wide + 1) % (2 * PLANE)
    up = (wide + 2 * PLANE - 1) % (2 * PLANE)
    beside = (wide + 2 * PLANE + 2 * core - 1) % (2 * PLANE)

    def plane_peer(i):
        return 2 * ((chip + i) % PLANE) + core

    def load_copy(x):
        return pltpu.make_async_copy(basis.at[:, x, :], stage.at[x], load_sem.at[x // 4])

    def loaded(group):
        part = stage.at[pl.ds(4 * group, 4)]
        pltpu.make_async_copy(part, part, load_sem.at[group]).wait()

    given = [
        pltpu.make_async_copy(far, near, in_sem.at[k])
        for k, (far, near) in enumerate((
            (given_coeffs, coeffs), (given_mean, mean), (given_vel, vel), (given_diff, diff), (given_reac, reac)
        ))
    ]

    barrier = pltpu.get_barrier_semaphore()

    def signal(to_wide, to_zed):
        pl.semaphore_signal(barrier, inc=1, device_id=(to_wide, to_zed), device_id_type=MESH)

    signal(partner, zed)
    signal(beside, zed)

    def greet_plane(i, carry):
        signal(plane_peer(i), zed)
        return carry

    lax.fori_loop(1, PLANE, greet_plane, 0)
    for i in range(1, DEPTH):
        signal(wide, (zed + i) % DEPTH)
    for c in given:
        c.start()
    for x in (*range(12, 16), *range(12)):
        load_copy(x).start()

    def remote(src, dst, send, recv, to_wide, to_zed):
        return pltpu.make_async_remote_copy(
            src_ref=src, dst_ref=dst, send_sem=send, recv_sem=recv,
            device_id=(to_wide, to_zed), device_id_type=MESH,
        )

    def over_plane(make, act):
        def body(i, carry):
            act(make(i))
            return carry

        lax.fori_loop(1, PLANE, body, 0)

    start = lambda c: c.start()
    wait_recv = lambda c: c.wait_recv()
    wait_send = lambda c: c.wait_send()

    def gather_out(g):
        def make(i):
            own = cbuf.at[g, chip, core]
            return remote(own, own, ag_send.at[g], ag_recv.at[g], plane_peer(i), zed)

        return make

    def gather_all(g):
        others = cbuf.at[g, 1:PLANE, 0]
        return remote(others, others, ag_send.at[g], ag_recv.at[g], partner, zed)

    def share(g, side):
        part = cbuf.at[g, :, side]
        return remote(part, part, agc_send.at[g], agc_recv.at[g], partner, zed)

    def gather_start(g):
        over_plane(gather_out(g), start)

    def gather_plane(g):
        gather_all(g).wait_recv()
        share(g, core).start()

    def gather_done(g):
        share(g, 1 - core).wait_recv()

    left = (zed + DEPTH - 1) % DEPTH
    right = (zed + 1) % DEPTH
    halos = (
        (vrow, vel.at[0, 8:16, :], vel.at[0, 0:8, :], 0),
        (mrow, mean.at[8:16, :], mean.at[0:8, :], 0),
        (vcol, vel.at[1, :, 128:256], vel.at[1, :, 0:128], 1),
        (mcol, mean.at[:, 128:256], mean.at[:, 0:128], 1),
        (halo_rows, edge_rows.at[0], edge_rows.at[1], 0),
        (halo_cols, edge_cols.at[0], edge_cols.at[1], 1),
    )

    def halo_start(k):
        held, first, second, sideways = halos[k]
        ahead, behind = ((wide, right), (wide, left)) if sideways else ((down, zed), (up, zed))
        remote(first, held.at[0], hal_send.at[k], hal_recv.at[k], *ahead).start()
        remote(second, held.at[1], hal_send.at[k], hal_recv.at[k], *behind).start()

    def halo_all(k):
        held = halos[k][0]
        return remote(held, held, hal_send.at[k], hal_recv.at[k], partner, zed)

    for c in given:
        c.wait()
    for g in range(2):
        cbuf[g, chip, core] = coeffs[:, g * HALF:(g + 1) * HALF]
    pl.semaphore_wait(barrier, 2 + PLANE - 1 + DEPTH - 1)
    gather_start(0)
    for k in range(4):
        halo_start(k)

    unit = (
        lax.broadcasted_iota(jnp.int32, (COLS, COLS), 0) == lax.broadcasted_iota(jnp.int32, (COLS, COLS), 1)
    ).astype(BF16)

    def prepare(x, edge):
        high, low = halves(stage[x])
        bn[x, :, 0:COLS] = high
        bn[x, :, COLS:2 * COLS] = low
        turn = lambda part: lax.dot_general(unit, part, (((1,), (1,)), ((), ())), preferred_element_type=F32)
        high = turn(high)
        low = turn(low)
        at = pl.ds(pl.multiple_of((x + 1) * COLS, COLS), COLS)
        bt[at, 0:MODES] = high.astype(BF16)
        bt[at, MODES:2 * MODES] = low.astype(BF16)
        if edge is not None:
            edge_rows[edge] = high + low
        edge_cols[0, x] = high[COLS - 1:COLS] + low[COLS - 1:COLS]
        edge_cols[1, x] = high[0:1] + low[0:1]

    def prepare_inner(x, carry):
        prepare(x, None)
        return carry

    loaded(3)
    prepare(ROWS - 1, 0)
    lax.fori_loop(12, ROWS - 1, prepare_inner, 0)
    loaded(0)
    prepare(0, 1)
    loaded(1)
    loaded(2)
    lax.fori_loop(1, 12, prepare_inner, 0)
    halo_start(5)
    gather_plane(0)
    halo_start(4)
    gather_start(1)

    def spread(cells, k):
        return jnp.broadcast_to(cells[:, k:k + 1], (cells.shape[0], 128))

    for k in range(4):
        halo_all(k).wait_recv()
    vx = vel[0]
    vy = vel[1]
    row_id = lax.broadcasted_iota(jnp.int32, (ROWS, COLS), 0)
    col_id = lax.broadcasted_iota(jnp.int32, (ROWS, COLS), 1)
    vx_next = jnp.where(row_id == ROWS - 1, jnp.broadcast_to(vrow[1, 0:1, :], (ROWS, COLS)), pltpu.roll(vx, ROWS - 1, 0))
    vx_prev = jnp.where(row_id == 0, jnp.broadcast_to(vrow[0, 7:8, :], (ROWS, COLS)), pltpu.roll(vx, 1, 0))
    vy_next = jnp.where(col_id == COLS - 1, jnp.broadcast_to(vcol[1, :, 0:1], (ROWS, COLS)), pltpu.roll(vy, COLS - 1, 1))
    vy_prev = jnp.where(col_id == 0, jnp.broadcast_to(vcol[0, :, 127:128], (ROWS, COLS)), pltpu.roll(vy, 1, 1))
    d = diff[...]
    zero_row = jnp.zeros((ROWS, COLS), F32)
    planes = (d - 0.5 * vx_next, d + 0.5 * vx_prev, d - 0.5 * vy_next, d + 0.5 * vy_prev, -4.0 * d, reac[...], mean[...], zero_row)
    for k, values in enumerate(planes):
        kc[0:ROWS, k, :] = values
        kc[ROWS:2 * ROWS, k, :] = zero_row
    kc[ROWS] = jnp.broadcast_to(mrow[0, 7:8, :], (8, COLS))
    kc[ROWS + 1] = jnp.broadcast_to(mrow[1, 0:1, :], (8, COLS))
    turned = kc[...].reshape(COLS, COLS).T
    for x in range(ROWS):
        tile = turned[:, 0:128]
        kx[x] = tile if x == 0 else pltpu.roll(tile, 128 - 8 * x, 1)
    mb[0:COLS, :] = spread(turned, 128)
    mb[EXT - COLS:EXT, :] = spread(turned, 136)
    mb[EXT:EXT + 16, :] = jnp.broadcast_to(mcol[0, :, 127:128], (16, 128))
    mb[EXT + 16:EXT + 32, :] = jnp.broadcast_to(mcol[1, :, 0:1], (16, 128))

    def spread_mean(x, carry):
        mb[pl.ds(pl.multiple_of((x + 1) * COLS, COLS), COLS), :] = spread(kx[x], 6)
        return carry

    lax.fori_loop(0, ROWS, spread_mean, 0)

    def spread_row(x):
        cells = kx[x]
        for k in range(6):
            ab[k, x] = spread(cells, k)

    shi = (shi_a, shi_b)
    slo = (slo_a, slo_b)

    def set_coeffs(g):
        high, low = halves(cbuf[g].reshape(MODES, HALF))
        chi[...] = high
        clo[...] = low

    def expand_rows(at, count):
        rows = bt[pl.ds(at, count), :]
        left_side = jnp.concatenate([rows, rows[:, 0:MODES]], axis=1)
        ch = chi[...]
        right_side = jnp.concatenate([ch, ch, clo[...]], axis=0)
        total = jnp.dot(left_side, right_side, preferred_element_type=F32)
        centre = mb[pl.ds(at, count), :]
        return [total[:, lt * 128:(lt + 1) * 128] + centre for lt in range(2)]

    def expand(i):
        at = pl.multiple_of(i * COLS, COLS)
        for lt, values in enumerate(expand_rows(at, COLS)):
            field[lt, i, PAD:PAD + COLS, :] = values

    def expand_pair(i):
        at = pl.multiple_of(i * COLS, COLS)
        for lt, values in enumerate(expand_rows(at, 2 * COLS)):
            for k in range(2):
                field[lt, i + k, PAD:PAD + COLS, :] = values[k * COLS:(k + 1) * COLS]

    def expand_sides():
        for lt, values in enumerate(expand_rows(EXT, 32)):
            for x in range(ROWS):
                field[lt, x + 1, PAD - 1:PAD, :] = values[x:x + 1]
                field[lt, x + 1, PAD + COLS:PAD + COLS + 1, :] = values[16 + x:17 + x]

    def source(r, slot, section, h):
        i = r + 1
        for lt in range(2):
            lanes = slice(lt * 128, (lt + 1) * 128)
            here = field[lt, i, PAD:PAD + COLS, :]
            total = ab[0, r] * field[lt, i + 1, PAD:PAD + COLS, :]
            total += ab[1, r] * field[lt, i - 1, PAD:PAD + COLS, :]
            total += ab[2, r] * field[lt, i, PAD + 1:PAD + COLS + 1, :]
            total += ab[3, r] * field[lt, i, PAD - 1:PAD + COLS - 1, :]
            total += ab[4, r] * here
            total += ab[5, r] * jnp.tanh(here)
            high, low = halves(total)
            shi[slot][:, lanes] = high
            slo[slot][:, lanes] = low
            if section == 0:
                tops = jnp.max(jnp.abs(here).reshape(COLS // 8, 8, 128), axis=0)
                peak[h, :, lanes] = jnp.maximum(peak[h, :, lanes], tops)

    def project(r, slot, n):
        sides = bn[r]
        left_side = jnp.concatenate([sides, sides[:, 0:COLS]], axis=1)
        sh = shi[slot][...]
        right_side = jnp.concatenate([sh, sh, slo[slot][...]], axis=0)
        part = jnp.dot(left_side, right_side, preferred_element_type=F32)
        pacc[n] = pacc[n] + part.reshape(PLANE, 2, 16, HALF)

    def section_of(section, h, early, hooks, before_rims):
        n = 2 * section + h
        prime = spread_row if n == 0 else lambda x: None
        prime(1)
        expand_sides()
        expand_pair(1)
        early()
        expand_pair(3)
        pacc[n] = jnp.zeros((PLANE, 2, 16, HALF), F32)
        if section == 0:
            peak[h] = jnp.zeros((8, HALF), F32)
        source(1, 1, section, h)
        prime(2)

        def body(r, carry):
            for at, hook in hooks:
                pl.when(r == at)(hook)
            project(2 * r + 1, 1, n)
            source(2 * r + 2, 0, section, h)
            prime(2 * r + 3)
            expand_pair(2 * r + 5)
            source(2 * r + 3, 1, section, h)
            prime(2 * r + 4)
            project(2 * r + 2, 0, n)
            return carry

        lax.fori_loop(0, ROWS // 2 - 2, body, 0)
        before_rims()
        prime(0)
        project(ROWS - 3, 1, n)
        source(ROWS - 2, 0, section, h)
        expand(0)
        project(ROWS - 2, 0, n)
        source(0, 1, section, h)
        prime(ROWS - 1)
        expand(ROWS + 1)
        project(0, 1, n)
        source(ROWS - 1, 0, section, h)
        project(ROWS - 1, 0, n)

    def core_out(n):
        return remote(pacc.at[n, :, 1 - core], rcore.at[n], core_send.at[n], core_recv.at[n], partner, zed)

    def peak_core(h):
        return remote(pcore.at[h, 0], pcore.at[h, 1], pkc_send.at[h], pkc_recv.at[h], partner, zed)

    def plane_out(n):
        def make(i):
            return remote(
                psum.at[n, (chip + i) % PLANE], rplane.at[n, i], pl_send.at[n], pl_recv.at[n], plane_peer(i), zed
            )

        return make

    def plane_all(n):
        return remote(psum.at[n, 1:PLANE], rplane.at[n, 1:PLANE], pl_send.at[n], pl_recv.at[n], partner, zed)

    def peak_plane(h):
        def make(i):
            return remote(pplane.at[h, 0], pplane.at[h, i], pkp_send.at[h], pkp_recv.at[h], plane_peer(i), zed)

        return make

    def peak_plane_all(h):
        others = pplane.at[h, 1:PLANE]
        return remote(others, others, pkp_send.at[h], pkp_recv.at[h], partner, zed)

    def z_start(n):
        mine = zbuf.at[n, zed]
        for i in range(1, DEPTH):
            remote(mine, mine, z_send.at[n], z_recv.at[n], wide, (zed + i) % DEPTH).start()

    def z_all(n):
        others = zbuf.at[n, 1:DEPTH]
        return remote(others, others, z_send.at[n], z_recv.at[n], partner, zed)

    def peak_z_start(h):
        for i in range(1, DEPTH):
            remote(pz.at[h, 0], pz.at[h, i], pkz_send.at[h], pkz_recv.at[h], wide, (zed + i) % DEPTH).start()

    def peak_z_all(h):
        others = pz.at[h, 1:DEPTH]
        return remote(others, others, pkz_send.at[h], pkz_recv.at[h], partner, zed)

    def sum_start(n):
        core_out(n).start()
        if n < 2:
            pcore[n, 0] = jnp.max(peak[n], axis=0, keepdims=True)
            peak_core(n).start()

    def sum_core(n):
        core_out(n).wait_recv()
        psum[n] = pacc[n, :, core] + rcore[n]
        over_plane(plane_out(n), start)
        if n < 2:
            peak_core(n).wait_recv()
            pplane[n, 0] = jnp.maximum(pcore[n, 0], pcore[n, 1])
            over_plane(peak_plane(n), start)

    def sum_plane(n):
        plane_all(n).wait_recv()
        total = psum[n, chip]
        for i in range(1, PLANE):
            total = total + rplane[n, i]
        zbuf[n, zed] = total
        z_start(n)
        if n < 2:
            peak_plane_all(n).wait_recv()
            top = pplane[n, 0]
            for i in range(1, PLANE):
                top = jnp.maximum(top, pplane[n, i])
            pz[n, 0] = top
            peak_z_start(n)

    def sum_z(n):
        h = n % 2
        lanes = slice(h * HALF, (h + 1) * HALF)
        z_all(n).wait_recv()
        total = weight * (((zbuf[n, 0] + zbuf[n, 1]) + zbuf[n, 2]) + zbuf[n, 3])
        if n < 2:
            peak_z_all(n).wait_recv()
            top = jnp.maximum(jnp.maximum(pz[n, 0], pz[n, 1]), jnp.maximum(pz[n, 2], pz[n, 3]))
            step = STEP_LIMIT / (1.0 + top)
            step_out[:, lanes] = jnp.broadcast_to(step, (16, HALF))
            rate_one[:, lanes] = total
            cbuf[2 + h, chip, core] = coeffs[:, lanes] + step * total
            gather_start(2 + h)
        else:
            rate_two[:, lanes] = total

    def split_into(values, at):
        high, low = halves(values)
        bt[at:at + values.shape[0], 0:MODES] = high
        bt[at:at + values.shape[0], MODES:2 * MODES] = low

    def rims():
        halo_all(4).wait_recv()
        for k, at in ((0, 0), (1, ROWS + 1)):
            for part in range(2):
                split_into(halo_rows[k, part * 128:(part + 1) * 128, :], at * COLS + part * 128)

    nothing = lambda: None
    halo_all(5).wait_recv()
    for k in range(2):
        split_into(halo_cols[k].reshape(ROWS, MODES), EXT + 16 * k)
    gather_done(0)
    set_coeffs(0)
    section_of(0, 0, nothing, ((5, lambda: gather_plane(1)),), rims)
    sum_start(0)
    gather_done(1)
    set_coeffs(1)
    section_of(0, 1, lambda: sum_core(0), ((4, lambda: sum_plane(0)),), nothing)
    sum_start(1)
    sum_z(0)
    sum_core(1)
    gather_plane(2)
    sum_plane(1)
    gather_done(2)
    set_coeffs(2)
    section_of(1, 0, nothing, ((1, lambda: sum_z(1)),), lambda: gather_plane(3))
    sum_start(2)
    gather_done(3)
    set_coeffs(3)
    section_of(1, 1, lambda: sum_core(2), ((4, lambda: sum_plane(2)),), nothing)
    sum_start(3)
    sum_z(2)
    sum_core(3)
    sum_plane(3)
    sum_z(3)

    for k in range(6):
        halo_all(k).wait_send()
    for g in range(4):
        for sent in (gather_all(g), share(g, core), core_out(g), plane_all(g), z_all(g)):
            sent.wait_send()
    for h in range(2):
        for sent in (peak_core(h), peak_plane_all(h), peak_z_all(h)):
            sent.wait_send()


def per_device(weight, coeffs, pod_basis, mean_field, velocity, diffusivity, reaction):
    vmem = lambda *shape: pltpu.VMEM(shape, F32)
    narrow = lambda *shape: pltpu.VMEM(shape, BF16)
    dma = lambda *shape: pltpu.SemaphoreType.DMA(shape)
    whole = pl.BlockSpec(memory_space=pltpu.VMEM)
    scratch = [
        vmem(16, TRAJ), vmem(ROWS, COLS), vmem(2, ROWS, COLS), vmem(ROWS, COLS), vmem(ROWS, COLS),
        vmem(ROWS, MODES, COLS),
        narrow(EXT + 32, 2 * MODES),
        narrow(ROWS, MODES, 2 * COLS),
        vmem(ROWS, COLS, 128),
        vmem(6, ROWS, COLS, 128),
        vmem(EXT + 32, 128),
        vmem(2, ROWS + 2, ROWPAD, 128),
        narrow(COLS, HALF),
        narrow(COLS, HALF),
        narrow(COLS, HALF),
        narrow(COLS, HALF),
        narrow(MODES, HALF),
        narrow(MODES, HALF),
        vmem(4, PLANE, 2, 16, HALF),
        vmem(4, PLANE, 16, HALF),
        vmem(4, PLANE, 16, HALF),
        vmem(4, PLANE, 16, HALF),
        vmem(4, DEPTH, 16, HALF),
        vmem(4, PLANE, 2, 16, HALF),
        vmem(2, COLS, MODES),
        vmem(2, COLS, MODES),
        vmem(2, ROWS, 1, MODES),
        vmem(2, ROWS, 1, MODES),
        vmem(2, 8, COLS),
        vmem(2, 8, COLS),
        vmem(2, ROWS, 128),
        vmem(2, ROWS, 128),
        vmem(2 * ROWS, 8, COLS),
        vmem(2, 8, HALF),
        vmem(2, 2, 1, HALF),
        vmem(2, PLANE, 1, HALF),
        vmem(2, DEPTH, 1, HALF),
        dma(5), dma(4),
        dma(4), dma(4), dma(4), dma(4),
        dma(6), dma(6), dma(4), dma(4),
        dma(4), dma(4), dma(4), dma(4),
        dma(2), dma(2), dma(2), dma(2), dma(2), dma(2),
    ]
    out = jax.ShapeDtypeStruct((16, TRAJ), F32)
    rate_one, rate_two, step_size = pl.pallas_call(
        functools.partial(kernel, weight),
        out_shape=(out, out, out),
        in_specs=[pl.BlockSpec(memory_space=pl.ANY)] * 6,
        out_specs=(whole, whole, whole),
        scratch_shapes=scratch,
        compiler_params=pltpu.CompilerParams(
            collective_id=0, has_side_effects=True, vmem_limit_bytes=67043328
        ),
    )(coeffs, pod_basis, mean_field, velocity, diffusivity, reaction)
    mean_rate = (rate_one + rate_two) * 0.5
    return coeffs + step_size * mean_rate, mean_rate


def solution(mesh):
    cells = ROWS * COLS * mesh.shape["wide"] * mesh.shape["col"]
    weight = math.sqrt(MODES / cells)
    placed = (
        P("wide", None),
        P(None, "wide", "col"),
        P("wide", "col"),
        P(None, "wide", "col"),
        P("wide", "col"),
        P("wide", "col"),
    )
    return jax.shard_map(
        functools.partial(per_device, weight),
        mesh=mesh,
        in_specs=placed,
        out_specs=(P("wide", None), P("wide", None)),
        check_vma=False,
    )
```

```python
import functools
import math

import jax
import jax.numpy as jnp
from jax import lax
from jax.experimental import pallas as pl
from jax.experimental.pallas import tpu as pltpu
from jax.sharding import PartitionSpec as P

MODES = 512
TRAJ = 512
ROWS = 16
COLS = 256
HALF = 256
PLANE = 16
DEPTH = 4
MESH = pl.DeviceIdType.MESH
F32 = jnp.float32
BF16 = jnp.bfloat16
STEP_LIMIT = 2.0
PAD = 8
ROWPAD = COLS + 2 * PAD
CELLS = ROWS * COLS
EXT = (ROWS + 2) * COLS


def halves(value):
    high = value.astype(BF16)
    return high, (value - high.astype(F32)).astype(BF16)


def kernel(
    weight,
    given_coeffs, basis, given_mean, given_vel, given_diff, given_reac,
    rate_one, rate_two, step_out,
    coeffs, mean, vel, diff, reac, stage, bt, bn, kx, ab, mb, field, shi_a, shi_b, slo_a, slo_b, chi, clo,
    pacc, psum, rcore, rplane, zbuf, cbuf,
    edge_rows, halo_rows, edge_cols, halo_cols,
    vrow, mrow, vcol, mcol, kc,
    peak, pcore, pplane, pz,
    in_sem, load_sem, ag_send, ag_recv, agc_send, agc_recv,
    hal_send, hal_recv, core_send, core_recv, pl_send, pl_recv, z_send, z_recv,
    pkc_send, pkc_recv, pkp_send, pkp_recv, pkz_send, pkz_recv,
):
    wide = lax.axis_index("wide")
    zed = lax.axis_index("col")
    chip = wide // 2
    core = wide % 2
    partner = wide + 1 - 2 * core
    down = (wide + 1) % (2 * PLANE)
    up = (wide + 2 * PLANE - 1) % (2 * PLANE)
    beside = (wide + 2 * PLANE + 2 * core - 1) % (2 * PLANE)

    def plane_peer(i):
        return 2 * ((chip + i) % PLANE) + core

    def load_copy(x):
        return pltpu.make_async_copy(basis.at[:, x, :], stage.at[x], load_sem.at[x // 4])

    def loaded(group):
        part = stage.at[pl.ds(4 * group, 4)]
        pltpu.make_async_copy(part, part, load_sem.at[group]).wait()

    given = [
        pltpu.make_async_copy(far, near, in_sem.at[k])
        for k, (far, near) in enumerate((
            (given_coeffs, coeffs), (given_mean, mean), (given_vel, vel), (given_diff, diff), (given_reac, reac)
        ))
    ]

    barrier = pltpu.get_barrier_semaphore()

    def signal(to_wide, to_zed):
        pl.semaphore_signal(barrier, inc=1, device_id=(to_wide, to_zed), device_id_type=MESH)

    signal(partner, zed)
    signal(beside, zed)

    def greet_plane(i, carry):
        signal(plane_peer(i), zed)
        return carry

    lax.fori_loop(1, PLANE, greet_plane, 0)
    for i in range(1, DEPTH):
        signal(wide, (zed + i) % DEPTH)
    for c in given:
        c.start()
    for x in (*range(12, 16), *range(12)):
        load_copy(x).start()

    def remote(src, dst, send, recv, to_wide, to_zed):
        return pltpu.make_async_remote_copy(
            src_ref=src, dst_ref=dst, send_sem=send, recv_sem=recv,
            device_id=(to_wide, to_zed), device_id_type=MESH,
        )

    def over_plane(make, act):
        def body(i, carry):
            act(make(i))
            return carry

        lax.fori_loop(1, PLANE, body, 0, unroll=True)

    start = lambda c: c.start()
    wait_recv = lambda c: c.wait_recv()
    wait_send = lambda c: c.wait_send()

    def gather_out(g):
        def make(i):
            own = cbuf.at[g, chip, core]
            return remote(own, own, ag_send.at[g], ag_recv.at[g], plane_peer(i), zed)

        return make

    def gather_all(g):
        others = cbuf.at[g, 1:PLANE, 0]
        return remote(others, others, ag_send.at[g], ag_recv.at[g], partner, zed)

    def share(g, side):
        part = cbuf.at[g, :, side]
        return remote(part, part, agc_send.at[g], agc_recv.at[g], partner, zed)

    def gather_start(g):
        over_plane(gather_out(g), start)

    def gather_plane(g):
        gather_all(g).wait_recv()
        share(g, core).start()

    def gather_done(g):
        share(g, 1 - core).wait_recv()

    left = (zed + DEPTH - 1) % DEPTH
    right = (zed + 1) % DEPTH
    halos = (
        (vrow, vel.at[0, 8:16, :], vel.at[0, 0:8, :], 0),
        (mrow, mean.at[8:16, :], mean.at[0:8, :], 0),
        (vcol, vel.at[1, :, 128:256], vel.at[1, :, 0:128], 1),
        (mcol, mean.at[:, 128:256], mean.at[:, 0:128], 1),
        (halo_rows, edge_rows.at[0], edge_rows.at[1], 0),
        (halo_cols, edge_cols.at[0], edge_cols.at[1], 1),
    )

    def halo_start(k):
        held, first, second, sideways = halos[k]
        ahead, behind = ((wide, right), (wide, left)) if sideways else ((down, zed), (up, zed))
        remote(first, held.at[0], hal_send.at[k], hal_recv.at[k], *ahead).start()
        remote(second, held.at[1], hal_send.at[k], hal_recv.at[k], *behind).start()

    def halo_all(k):
        held = halos[k][0]
        return remote(held, held, hal_send.at[k], hal_recv.at[k], partner, zed)

    for c in given:
        c.wait()
    for g in range(2):
        cbuf[g, chip, core] = coeffs[:, g * HALF:(g + 1) * HALF]

    unit = (
        lax.broadcasted_iota(jnp.int32, (COLS, COLS), 0) == lax.broadcasted_iota(jnp.int32, (COLS, COLS), 1)
    ).astype(BF16)

    def prepare(x, edge):
        high, low = halves(stage[x])
        bn[x, :, 0:COLS] = high
        bn[x, :, COLS:2 * COLS] = low
        turn = lambda part: lax.dot_general(unit, part, (((1,), (1,)), ((), ())), preferred_element_type=F32)
        high = turn(high)
        low = turn(low)
        at = pl.ds(pl.multiple_of((x + 1) * COLS, COLS), COLS)
        bt[at, 0:MODES] = high.astype(BF16)
        bt[at, MODES:2 * MODES] = low.astype(BF16)
        if edge is not None:
            edge_rows[edge] = high + low
        edge_cols[0, x] = high[COLS - 1:COLS] + low[COLS - 1:COLS]
        edge_cols[1, x] = high[0:1] + low[0:1]

    def prepare_inner(x, carry):
        prepare(x, None)
        return carry

    loaded(3)
    prepare(ROWS - 1, 0)
    lax.fori_loop(12, ROWS - 1, prepare_inner, 0)
    pl.semaphore_wait(barrier, 2 + PLANE - 1 + DEPTH - 1)
    gather_start(0)
    for k in range(4):
        halo_start(k)

    loaded(0)
    prepare(0, 1)
    halo_start(4)
    loaded(1)
    loaded(2)
    lax.fori_loop(1, 12, prepare_inner, 0)
    halo_start(5)
    gather_plane(0)
    gather_start(1)

    def spread(cells, k):
        return jnp.broadcast_to(cells[:, k:k + 1], (cells.shape[0], 128))

    for k in range(4):
        halo_all(k).wait_recv()
    vx = vel[0]
    vy = vel[1]
    row_id = lax.broadcasted_iota(jnp.int32, (ROWS, COLS), 0)
    col_id = lax.broadcasted_iota(jnp.int32, (ROWS, COLS), 1)
    vx_next = jnp.where(row_id == ROWS - 1, jnp.broadcast_to(vrow[1, 0:1, :], (ROWS, COLS)), pltpu.roll(vx, ROWS - 1, 0))
    vx_prev = jnp.where(row_id == 0, jnp.broadcast_to(vrow[0, 7:8, :], (ROWS, COLS)), pltpu.roll(vx, 1, 0))
    vy_next = jnp.where(col_id == COLS - 1, jnp.broadcast_to(vcol[1, :, 0:1], (ROWS, COLS)), pltpu.roll(vy, COLS - 1, 1))
    vy_prev = jnp.where(col_id == 0, jnp.broadcast_to(vcol[0, :, 127:128], (ROWS, COLS)), pltpu.roll(vy, 1, 1))
    d = diff[...]
    zero_row = jnp.zeros((ROWS, COLS), F32)
    planes = (d - 0.5 * vx_next, d + 0.5 * vx_prev, d - 0.5 * vy_next, d + 0.5 * vy_prev, -4.0 * d, reac[...], mean[...], zero_row)
    for k, values in enumerate(planes):
        kc[0:ROWS, k, :] = values
        kc[ROWS:2 * ROWS, k, :] = zero_row
    kc[ROWS] = jnp.broadcast_to(mrow[0, 7:8, :], (8, COLS))
    kc[ROWS + 1] = jnp.broadcast_to(mrow[1, 0:1, :], (8, COLS))
    turned = kc[...].reshape(COLS, COLS).T
    for x in range(ROWS):
        tile = turned[:, 0:128]
        kx[x] = tile if x == 0 else pltpu.roll(tile, 128 - 8 * x, 1)
    mb[0:COLS, :] = spread(turned, 128)
    mb[EXT - COLS:EXT, :] = spread(turned, 136)
    mb[EXT:EXT + 16, :] = jnp.broadcast_to(mcol[0, :, 127:128], (16, 128))
    mb[EXT + 16:EXT + 32, :] = jnp.broadcast_to(mcol[1, :, 0:1], (16, 128))

    def spread_mean(x, carry):
        mb[pl.ds(pl.multiple_of((x + 1) * COLS, COLS), COLS), :] = spread(kx[x], 6)
        return carry

    lax.fori_loop(0, ROWS, spread_mean, 0)

    def spread_row(x):
        cells = kx[x]
        for k in range(6):
            ab[k, x] = spread(cells, k)

    shi = (shi_a, shi_b)
    slo = (slo_a, slo_b)

    def set_coeffs(g):
        high, low = halves(cbuf[g].reshape(MODES, HALF))
        chi[...] = high
        clo[...] = low

    def expand_rows(at, count):
        rows = bt[pl.ds(at, count), :]
        left_side = jnp.concatenate([rows, rows[:, 0:MODES]], axis=1)
        ch = chi[...]
        right_side = jnp.concatenate([ch, ch, clo[...]], axis=0)
        total = jnp.dot(left_side, right_side, preferred_element_type=F32)
        centre = mb[pl.ds(at, count), :]
        return [total[:, lt * 128:(lt + 1) * 128] + centre for lt in range(2)]

    def expand(i):
        at = pl.multiple_of(i * COLS, COLS)
        for lt, values in enumerate(expand_rows(at, COLS)):
            field[lt, i, PAD:PAD + COLS, :] = values

    def expand_pair(i):
        at = pl.multiple_of(i * COLS, COLS)
        for lt, values in enumerate(expand_rows(at, 2 * COLS)):
            for k in range(2):
                field[lt, i + k, PAD:PAD + COLS, :] = values[k * COLS:(k + 1) * COLS]

    def expand_sides():
        for lt, values in enumerate(expand_rows(EXT, 32)):
            for x in range(ROWS):
                field[lt, x + 1, PAD - 1:PAD, :] = values[x:x + 1]
                field[lt, x + 1, PAD + COLS:PAD + COLS + 1, :] = values[16 + x:17 + x]

    def source(r, slot, section, h):
        i = r + 1
        for lt in range(2):
            lanes = slice(lt * 128, (lt + 1) * 128)
            here = field[lt, i, PAD:PAD + COLS, :]
            total = ab[0, r] * field[lt, i + 1, PAD:PAD + COLS, :]
            total += ab[1, r] * field[lt, i - 1, PAD:PAD + COLS, :]
            total += ab[2, r] * field[lt, i, PAD + 1:PAD + COLS + 1, :]
            total += ab[3, r] * field[lt, i, PAD - 1:PAD + COLS - 1, :]
            total += ab[4, r] * here
            total += ab[5, r] * jnp.tanh(here)
            high, low = halves(total)
            shi[slot][:, lanes] = high
            slo[slot][:, lanes] = low
            if section == 0:
                tops = jnp.max(jnp.abs(here).reshape(COLS // 8, 8, 128), axis=0)
                peak[h, :, lanes] = jnp.maximum(peak[h, :, lanes], tops)

    def project(r, slot, n):
        sides = bn[r]
        left_side = jnp.concatenate([sides, sides[:, 0:COLS]], axis=1)
        sh = shi[slot][...]
        right_side = jnp.concatenate([sh, sh, slo[slot][...]], axis=0)
        part = jnp.dot(left_side, right_side, preferred_element_type=F32)
        pacc[n] = pacc[n] + part.reshape(PLANE, 2, 16, HALF)

    def section_of(section, h, early, hooks, before_rims):
        n = 2 * section + h
        prime = spread_row if n == 0 else lambda x: None
        prime(1)
        expand_sides()
        expand_pair(1)
        early()
        expand_pair(3)
        pacc[n] = jnp.zeros((PLANE, 2, 16, HALF), F32)
        if section == 0:
            peak[h] = jnp.zeros((8, HALF), F32)
        source(1, 1, section, h)
        prime(2)

        def body(r, carry):
            for at, hook in hooks:
                pl.when(r == at)(hook)
            project(2 * r + 1, 1, n)
            source(2 * r + 2, 0, section, h)
            prime(2 * r + 3)
            expand_pair(2 * r + 5)
            source(2 * r + 3, 1, section, h)
            prime(2 * r + 4)
            project(2 * r + 2, 0, n)
            return carry

        lax.fori_loop(0, ROWS // 2 - 2, body, 0)
        before_rims()
        prime(0)
        project(ROWS - 3, 1, n)
        source(ROWS - 2, 0, section, h)
        expand(0)
        project(ROWS - 2, 0, n)
        source(0, 1, section, h)
        prime(ROWS - 1)
        expand(ROWS + 1)
        project(0, 1, n)
        source(ROWS - 1, 0, section, h)
        project(ROWS - 1, 0, n)

    def core_out(n):
        return remote(pacc.at[n, :, 1 - core], rcore.at[n], core_send.at[n], core_recv.at[n], partner, zed)

    def peak_core(h):
        return remote(pcore.at[h, 0], pcore.at[h, 1], pkc_send.at[h], pkc_recv.at[h], partner, zed)

    def plane_out(n):
        def make(i):
            return remote(
                psum.at[n, (chip + i) % PLANE], rplane.at[n, i], pl_send.at[n], pl_recv.at[n], plane_peer(i), zed
            )

        return make

    def plane_all(n):
        return remote(psum.at[n, 1:PLANE], rplane.at[n, 1:PLANE], pl_send.at[n], pl_recv.at[n], partner, zed)

    def peak_plane(h):
        def make(i):
            return remote(pplane.at[h, 0], pplane.at[h, i], pkp_send.at[h], pkp_recv.at[h], plane_peer(i), zed)

        return make

    def peak_plane_all(h):
        others = pplane.at[h, 1:PLANE]
        return remote(others, others, pkp_send.at[h], pkp_recv.at[h], partner, zed)

    def z_start(n):
        mine = zbuf.at[n, zed]
        for i in range(1, DEPTH):
            remote(mine, mine, z_send.at[n], z_recv.at[n], wide, (zed + i) % DEPTH).start()

    def z_all(n):
        others = zbuf.at[n, 1:DEPTH]
        return remote(others, others, z_send.at[n], z_recv.at[n], partner, zed)

    def peak_z_start(h):
        for i in range(1, DEPTH):
            remote(pz.at[h, 0], pz.at[h, i], pkz_send.at[h], pkz_recv.at[h], wide, (zed + i) % DEPTH).start()

    def peak_z_all(h):
        others = pz.at[h, 1:DEPTH]
        return remote(others, others, pkz_send.at[h], pkz_recv.at[h], partner, zed)

    def sum_start(n):
        core_out(n).start()
        if n < 2:
            pcore[n, 0] = jnp.max(peak[n], axis=0, keepdims=True)
            peak_core(n).start()

    def sum_core(n):
        core_out(n).wait_recv()
        psum[n] = pacc[n, :, core] + rcore[n]
        over_plane(plane_out(n), start)
        if n < 2:
            peak_core(n).wait_recv()
            pplane[n, 0] = jnp.maximum(pcore[n, 0], pcore[n, 1])
            over_plane(peak_plane(n), start)

    def sum_plane(n):
        plane_all(n).wait_recv()
        total = psum[n, chip]
        for i in range(1, PLANE):
            total = total + rplane[n, i]
        zbuf[n, zed] = total
        z_start(n)
        if n < 2:
            peak_plane_all(n).wait_recv()
            top = pplane[n, 0]
            for i in range(1, PLANE):
                top = jnp.maximum(top, pplane[n, i])
            pz[n, 0] = top
            peak_z_start(n)

    def sum_z(n):
        h = n % 2
        lanes = slice(h * HALF, (h + 1) * HALF)
        z_all(n).wait_recv()
        total = weight * (((zbuf[n, 0] + zbuf[n, 1]) + zbuf[n, 2]) + zbuf[n, 3])
        if n < 2:
            peak_z_all(n).wait_recv()
            top = jnp.maximum(jnp.maximum(pz[n, 0], pz[n, 1]), jnp.maximum(pz[n, 2], pz[n, 3]))
            step = STEP_LIMIT / (1.0 + top)
            step_out[:, lanes] = jnp.broadcast_to(step, (16, HALF))
            rate_one[:, lanes] = total
            cbuf[2 + h, chip, core] = coeffs[:, lanes] + step * total
            gather_start(2 + h)
        else:
            rate_two[:, lanes] = total

    def split_into(values, at):
        high, low = halves(values)
        bt[at:at + values.shape[0], 0:MODES] = high
        bt[at:at + values.shape[0], MODES:2 * MODES] = low

    def rims():
        halo_all(4).wait_recv()
        for k, at in ((0, 0), (1, ROWS + 1)):
            for part in range(2):
                split_into(halo_rows[k, part * 128:(part + 1) * 128, :], at * COLS + part * 128)

    nothing = lambda: None
    halo_all(5).wait_recv()
    for k in range(2):
        split_into(halo_cols[k].reshape(ROWS, MODES), EXT + 16 * k)
    gather_done(0)
    set_coeffs(0)
    section_of(0, 0, nothing, ((5, lambda: gather_plane(1)),), rims)
    sum_start(0)
    gather_done(1)
    set_coeffs(1)
    section_of(0, 1, lambda: sum_core(0), ((4, lambda: sum_plane(0)),), nothing)
    sum_start(1)
    sum_z(0)
    sum_core(1)
    gather_plane(2)
    sum_plane(1)
    gather_done(2)
    set_coeffs(2)
    section_of(1, 0, nothing, ((1, lambda: sum_z(1)),), lambda: gather_plane(3))
    sum_start(2)
    gather_done(3)
    set_coeffs(3)
    section_of(1, 1, nothing, ((0, lambda: sum_core(2)), (5, lambda: sum_plane(2))), nothing)
    sum_start(3)
    sum_core(3)
    sum_z(2)
    sum_plane(3)
    sum_z(3)

    for k in range(6):
        halo_all(k).wait_send()
    for g in range(4):
        for sent in (gather_all(g), share(g, core), core_out(g), plane_all(g), z_all(g)):
            sent.wait_send()
    for h in range(2):
        for sent in (peak_core(h), peak_plane_all(h), peak_z_all(h)):
            sent.wait_send()


def per_device(weight, coeffs, pod_basis, mean_field, velocity, diffusivity, reaction):
    vmem = lambda *shape: pltpu.VMEM(shape, F32)
    narrow = lambda *shape: pltpu.VMEM(shape, BF16)
    dma = lambda *shape: pltpu.SemaphoreType.DMA(shape)
    whole = pl.BlockSpec(memory_space=pltpu.VMEM)
    scratch = [
        vmem(16, TRAJ), vmem(ROWS, COLS), vmem(2, ROWS, COLS), vmem(ROWS, COLS), vmem(ROWS, COLS),
        vmem(ROWS, MODES, COLS),
        narrow(EXT + 32, 2 * MODES),
        narrow(ROWS, MODES, 2 * COLS),
        vmem(ROWS, COLS, 128),
        vmem(6, ROWS, COLS, 128),
        vmem(EXT + 32, 128),
        vmem(2, ROWS + 2, ROWPAD, 128),
        narrow(COLS, HALF),
        narrow(COLS, HALF),
        narrow(COLS, HALF),
        narrow(COLS, HALF),
        narrow(MODES, HALF),
        narrow(MODES, HALF),
        vmem(4, PLANE, 2, 16, HALF),
        vmem(4, PLANE, 16, HALF),
        vmem(4, PLANE, 16, HALF),
        vmem(4, PLANE, 16, HALF),
        vmem(4, DEPTH, 16, HALF),
        vmem(4, PLANE, 2, 16, HALF),
        vmem(2, COLS, MODES),
        vmem(2, COLS, MODES),
        vmem(2, ROWS, 1, MODES),
        vmem(2, ROWS, 1, MODES),
        vmem(2, 8, COLS),
        vmem(2, 8, COLS),
        vmem(2, ROWS, 128),
        vmem(2, ROWS, 128),
        vmem(2 * ROWS, 8, COLS),
        vmem(2, 8, HALF),
        vmem(2, 2, 1, HALF),
        vmem(2, PLANE, 1, HALF),
        vmem(2, DEPTH, 1, HALF),
        dma(5), dma(4),
        dma(4), dma(4), dma(4), dma(4),
        dma(6), dma(6), dma(4), dma(4),
        dma(4), dma(4), dma(4), dma(4),
        dma(2), dma(2), dma(2), dma(2), dma(2), dma(2),
    ]
    out = jax.ShapeDtypeStruct((16, TRAJ), F32)
    rate_one, rate_two, step_size = pl.pallas_call(
        functools.partial(kernel, weight),
        out_shape=(out, out, out),
        in_specs=[pl.BlockSpec(memory_space=pl.ANY)] * 6,
        out_specs=(whole, whole, whole),
        scratch_shapes=scratch,
        compiler_params=pltpu.CompilerParams(
            collective_id=0, has_side_effects=True, vmem_limit_bytes=67043328
        ),
    )(coeffs, pod_basis, mean_field, velocity, diffusivity, reaction)
    mean_rate = (rate_one + rate_two) * 0.5
    return coeffs + step_size * mean_rate, mean_rate


def solution(mesh):
    cells = ROWS * COLS * mesh.shape["wide"] * mesh.shape["col"]
    weight = math.sqrt(MODES / cells)
    placed = (
        P("wide", None),
        P(None, "wide", "col"),
        P("wide", "col"),
        P(None, "wide", "col"),
        P("wide", "col"),
        P("wide", "col"),
    )
    return jax.shard_map(
        functools.partial(per_device, weight),
        mesh=mesh,
        in_specs=placed,
        out_specs=(P("wide", None), P("wide", None)),
        check_vma=False,
    )
```

```python
import functools
import math

import jax
import jax.numpy as jnp
from jax import lax
from jax.experimental import pallas as pl
from jax.experimental.pallas import tpu as pltpu
from jax.sharding import PartitionSpec as P

MODES = 512
TRAJ = 512
ROWS = 16
COLS = 256
HALF = 256
PLANE = 16
DEPTH = 4
MESH = pl.DeviceIdType.MESH
F32 = jnp.float32
BF16 = jnp.bfloat16
STEP_LIMIT = 2.0
PAD = 8
ROWPAD = COLS + 2 * PAD
CELLS = ROWS * COLS
EXT = (ROWS + 2) * COLS


def halves(value):
    high = value.astype(BF16)
    return high, (value - high.astype(F32)).astype(BF16)


def kernel(
    weight,
    given_coeffs, basis, given_mean, given_vel, given_diff, given_reac,
    rate_one, rate_two, step_out,
    coeffs, mean, vel, diff, reac, stage, bt, bn, kx, ab, mb, field, shi_a, shi_b, slo_a, slo_b, chi, clo,
    pacc, psum, rcore, rplane, zbuf, cbuf,
    edge_rows, halo_rows, edge_cols, halo_cols,
    vrow, mrow, vcol, mcol, kc,
    peak, pcore, pplane, pz,
    in_sem, load_sem, ag_send, ag_recv, agc_send, agc_recv,
    hal_send, hal_recv, core_send, core_recv, pl_send, pl_recv, z_send, z_recv,
    pkc_send, pkc_recv, pkp_send, pkp_recv, pkz_send, pkz_recv,
):
    wide = lax.axis_index("wide")
    zed = lax.axis_index("col")
    chip = wide // 2
    core = wide % 2
    partner = wide + 1 - 2 * core
    down = (wide + 1) % (2 * PLANE)
    up = (wide + 2 * PLANE - 1) % (2 * PLANE)
    beside = (wide + 2 * PLANE + 2 * core - 1) % (2 * PLANE)

    def plane_peer(i):
        return 2 * ((chip + i) % PLANE) + core

    def load_copy(x):
        return pltpu.make_async_copy(basis.at[:, x, :], stage.at[x], load_sem.at[x // 4])

    def loaded(group):
        part = stage.at[pl.ds(4 * group, 4)]
        pltpu.make_async_copy(part, part, load_sem.at[group]).wait()

    given = [
        pltpu.make_async_copy(far, near, in_sem.at[k])
        for k, (far, near) in enumerate((
            (given_coeffs, coeffs), (given_mean, mean), (given_vel, vel), (given_diff, diff), (given_reac, reac)
        ))
    ]

    barrier = pltpu.get_barrier_semaphore()

    def signal(to_wide, to_zed):
        pl.semaphore_signal(barrier, inc=1, device_id=(to_wide, to_zed), device_id_type=MESH)

    signal(partner, zed)
    signal(beside, zed)

    def greet_plane(i, carry):
        signal(plane_peer(i), zed)
        return carry

    lax.fori_loop(1, PLANE, greet_plane, 0)
    for i in range(1, DEPTH):
        signal(wide, (zed + i) % DEPTH)
    for c in given:
        c.start()
    for x in (*range(12, 16), *range(12)):
        load_copy(x).start()

    def remote(src, dst, send, recv, to_wide, to_zed):
        return pltpu.make_async_remote_copy(
            src_ref=src, dst_ref=dst, send_sem=send, recv_sem=recv,
            device_id=(to_wide, to_zed), device_id_type=MESH,
        )

    def over_plane(make, act):
        def body(i, carry):
            act(make(i))
            return carry

        lax.fori_loop(1, PLANE, body, 0, unroll=True)

    start = lambda c: c.start()
    wait_recv = lambda c: c.wait_recv()
    wait_send = lambda c: c.wait_send()

    def gather_out(g):
        def make(i):
            own = cbuf.at[g, chip, core]
            return remote(own, own, ag_send.at[g], ag_recv.at[g], plane_peer(i), zed)

        return make

    def gather_all(g):
        others = cbuf.at[g, 1:PLANE, 0]
        return remote(others, others, ag_send.at[g], ag_recv.at[g], partner, zed)

    def share(g, side):
        part = cbuf.at[g, :, side]
        return remote(part, part, agc_send.at[g], agc_recv.at[g], partner, zed)

    def gather_start(g):
        over_plane(gather_out(g), start)

    def gather_plane(g):
        gather_all(g).wait_recv()
        share(g, core).start()

    def gather_done(g):
        share(g, 1 - core).wait_recv()

    left = (zed + DEPTH - 1) % DEPTH
    right = (zed + 1) % DEPTH
    halos = (
        (vrow, vel.at[0, 8:16, :], vel.at[0, 0:8, :], 0),
        (mrow, mean.at[8:16, :], mean.at[0:8, :], 0),
        (vcol, vel.at[1, :, 128:256], vel.at[1, :, 0:128], 1),
        (mcol, mean.at[:, 128:256], mean.at[:, 0:128], 1),
        (halo_rows, edge_rows.at[0], edge_rows.at[1], 0),
        (halo_cols, edge_cols.at[0], edge_cols.at[1], 1),
    )

    def halo_start(k):
        held, first, second, sideways = halos[k]
        ahead, behind = ((wide, right), (wide, left)) if sideways else ((down, zed), (up, zed))
        remote(first, held.at[0], hal_send.at[k], hal_recv.at[k], *ahead).start()
        remote(second, held.at[1], hal_send.at[k], hal_recv.at[k], *behind).start()

    def halo_all(k):
        held = halos[k][0]
        return remote(held, held, hal_send.at[k], hal_recv.at[k], partner, zed)

    for c in given:
        c.wait()
    for g in range(2):
        cbuf[g, chip, core] = coeffs[:, g * HALF:(g + 1) * HALF]

    unit = (
        lax.broadcasted_iota(jnp.int32, (COLS, COLS), 0) == lax.broadcasted_iota(jnp.int32, (COLS, COLS), 1)
    ).astype(BF16)

    def prepare(x, edge):
        high, low = halves(stage[x])
        bn[x, :, 0:COLS] = high
        bn[x, :, COLS:2 * COLS] = low
        turn = lambda part: lax.dot_general(unit, part, (((1,), (1,)), ((), ())), preferred_element_type=F32)
        high = turn(high)
        low = turn(low)
        at = pl.ds(pl.multiple_of((x + 1) * COLS, COLS), COLS)
        bt[at, 0:MODES] = high.astype(BF16)
        bt[at, MODES:2 * MODES] = low.astype(BF16)
        if edge is not None:
            edge_rows[edge] = high + low
        edge_cols[0, x] = high[COLS - 1:COLS] + low[COLS - 1:COLS]
        edge_cols[1, x] = high[0:1] + low[0:1]

    def prepare_inner(x, carry):
        prepare(x, None)
        return carry

    loaded(3)
    prepare(ROWS - 1, 0)
    lax.fori_loop(12, ROWS - 1, prepare_inner, 0)
    pl.semaphore_wait(barrier, 2 + PLANE - 1 + DEPTH - 1)
    gather_start(0)
    for k in range(4):
        halo_start(k)

    loaded(0)
    prepare(0, 1)
    halo_start(4)
    loaded(1)
    loaded(2)
    lax.fori_loop(1, 12, prepare_inner, 0)
    halo_start(5)
    gather_plane(0)
    gather_start(1)

    def spread(cells, k):
        return jnp.broadcast_to(cells[:, k:k + 1], (cells.shape[0], 128))

    for k in range(4):
        halo_all(k).wait_recv()
    vx = vel[0]
    vy = vel[1]
    row_id = lax.broadcasted_iota(jnp.int32, (ROWS, COLS), 0)
    col_id = lax.broadcasted_iota(jnp.int32, (ROWS, COLS), 1)
    vx_next = jnp.where(row_id == ROWS - 1, jnp.broadcast_to(vrow[1, 0:1, :], (ROWS, COLS)), pltpu.roll(vx, ROWS - 1, 0))
    vx_prev = jnp.where(row_id == 0, jnp.broadcast_to(vrow[0, 7:8, :], (ROWS, COLS)), pltpu.roll(vx, 1, 0))
    vy_next = jnp.where(col_id == COLS - 1, jnp.broadcast_to(vcol[1, :, 0:1], (ROWS, COLS)), pltpu.roll(vy, COLS - 1, 1))
    vy_prev = jnp.where(col_id == 0, jnp.broadcast_to(vcol[0, :, 127:128], (ROWS, COLS)), pltpu.roll(vy, 1, 1))
    d = diff[...]
    zero_row = jnp.zeros((ROWS, COLS), F32)
    planes = (d - 0.5 * vx_next, d + 0.5 * vx_prev, d - 0.5 * vy_next, d + 0.5 * vy_prev, -4.0 * d, reac[...], mean[...], zero_row)
    for k, values in enumerate(planes):
        kc[0:ROWS, k, :] = values
        kc[ROWS:2 * ROWS, k, :] = zero_row
    kc[ROWS] = jnp.broadcast_to(mrow[0, 7:8, :], (8, COLS))
    kc[ROWS + 1] = jnp.broadcast_to(mrow[1, 0:1, :], (8, COLS))
    turned = kc[...].reshape(COLS, COLS).T
    for x in range(ROWS):
        tile = turned[:, 0:128]
        kx[x] = tile if x == 0 else pltpu.roll(tile, 128 - 8 * x, 1)
    mb[0:COLS, :] = spread(turned, 128)
    mb[EXT - COLS:EXT, :] = spread(turned, 136)
    mb[EXT:EXT + 16, :] = jnp.broadcast_to(mcol[0, :, 127:128], (16, 128))
    mb[EXT + 16:EXT + 32, :] = jnp.broadcast_to(mcol[1, :, 0:1], (16, 128))

    def spread_mean(x, carry):
        mb[pl.ds(pl.multiple_of((x + 1) * COLS, COLS), COLS), :] = spread(kx[x], 6)
        return carry

    lax.fori_loop(0, ROWS, spread_mean, 0)

    def spread_row(x):
        cells = kx[x]
        for k in range(6):
            ab[k, x] = spread(cells, k)

    shi = (shi_a, shi_b)
    slo = (slo_a, slo_b)

    def set_coeffs(g):
        high, low = halves(cbuf[g].reshape(MODES, HALF))
        chi[...] = high
        clo[...] = low

    def expand_rows(at, count):
        rows = bt[pl.ds(at, count), :]
        left_side = jnp.concatenate([rows, rows[:, 0:MODES]], axis=1)
        ch = chi[...]
        right_side = jnp.concatenate([ch, ch, clo[...]], axis=0)
        total = jnp.dot(left_side, right_side, preferred_element_type=F32)
        centre = mb[pl.ds(at, count), :]
        return [total[:, lt * 128:(lt + 1) * 128] + centre for lt in range(2)]

    def expand(i):
        at = pl.multiple_of(i * COLS, COLS)
        for lt, values in enumerate(expand_rows(at, COLS)):
            field[lt, i, PAD:PAD + COLS, :] = values

    def expand_pair(i):
        at = pl.multiple_of(i * COLS, COLS)
        for lt, values in enumerate(expand_rows(at, 2 * COLS)):
            for k in range(2):
                field[lt, i + k, PAD:PAD + COLS, :] = values[k * COLS:(k + 1) * COLS]

    def expand_sides():
        for lt, values in enumerate(expand_rows(EXT, 32)):
            for x in range(ROWS):
                field[lt, x + 1, PAD - 1:PAD, :] = values[x:x + 1]
                field[lt, x + 1, PAD + COLS:PAD + COLS + 1, :] = values[16 + x:17 + x]

    def source(r, slot, section, h):
        i = r + 1
        for lt in range(2):
            lanes = slice(lt * 128, (lt + 1) * 128)
            here = field[lt, i, PAD:PAD + COLS, :]
            total = ab[0, r] * field[lt, i + 1, PAD:PAD + COLS, :]
            total += ab[1, r] * field[lt, i - 1, PAD:PAD + COLS, :]
            total += ab[2, r] * field[lt, i, PAD + 1:PAD + COLS + 1, :]
            total += ab[3, r] * field[lt, i, PAD - 1:PAD + COLS - 1, :]
            total += ab[4, r] * here
            total += ab[5, r] * jnp.tanh(here)
            high, low = halves(total)
            shi[slot][:, lanes] = high
            slo[slot][:, lanes] = low
            if section == 0:
                tops = jnp.max(jnp.abs(here).reshape(COLS // 8, 8, 128), axis=0)
                peak[h, :, lanes] = jnp.maximum(peak[h, :, lanes], tops)

    def project(r, slot, n):
        sides = bn[r]
        left_side = jnp.concatenate([sides, sides[:, 0:COLS]], axis=1)
        sh = shi[slot][...]
        right_side = jnp.concatenate([sh, sh, slo[slot][...]], axis=0)
        part = jnp.dot(left_side, right_side, preferred_element_type=F32)
        pacc[n] = pacc[n] + part.reshape(PLANE, 2, 16, HALF)

    def section_of(section, h, early, hooks, before_rims):
        n = 2 * section + h
        prime = spread_row if n == 0 else lambda x: None
        prime(1)
        expand_sides()
        expand_pair(1)
        early()
        expand_pair(3)
        pacc[n] = jnp.zeros((PLANE, 2, 16, HALF), F32)
        if section == 0:
            peak[h] = jnp.zeros((8, HALF), F32)
        source(1, 1, section, h)
        prime(2)

        def body(r, carry):
            for at, hook in hooks:
                pl.when(r == at)(hook)
            project(2 * r + 1, 1, n)
            source(2 * r + 2, 0, section, h)
            prime(2 * r + 3)
            expand_pair(2 * r + 5)
            source(2 * r + 3, 1, section, h)
            prime(2 * r + 4)
            project(2 * r + 2, 0, n)
            return carry

        lax.fori_loop(0, ROWS // 2 - 2, body, 0)
        before_rims()
        prime(0)
        project(ROWS - 3, 1, n)
        source(ROWS - 2, 0, section, h)
        expand(0)
        project(ROWS - 2, 0, n)
        source(0, 1, section, h)
        prime(ROWS - 1)
        expand(ROWS + 1)
        project(0, 1, n)
        source(ROWS - 1, 0, section, h)
        project(ROWS - 1, 0, n)

    def core_out(n):
        return remote(pacc.at[n, :, 1 - core], rcore.at[n], core_send.at[n], core_recv.at[n], partner, zed)

    def peak_core(h):
        return remote(pcore.at[h, 0], pcore.at[h, 1], pkc_send.at[h], pkc_recv.at[h], partner, zed)

    def plane_out(n):
        def make(i):
            return remote(
                psum.at[n, (chip + i) % PLANE], rplane.at[n, i], pl_send.at[n], pl_recv.at[n], plane_peer(i), zed
            )

        return make

    def plane_all(n):
        return remote(psum.at[n, 1:PLANE], rplane.at[n, 1:PLANE], pl_send.at[n], pl_recv.at[n], partner, zed)

    def peak_plane(h):
        def make(i):
            return remote(pplane.at[h, 0], pplane.at[h, i], pkp_send.at[h], pkp_recv.at[h], plane_peer(i), zed)

        return make

    def peak_plane_all(h):
        others = pplane.at[h, 1:PLANE]
        return remote(others, others, pkp_send.at[h], pkp_recv.at[h], partner, zed)

    def z_start(n):
        mine = zbuf.at[n, zed]
        for i in range(1, DEPTH):
            remote(mine, mine, z_send.at[n], z_recv.at[n], wide, (zed + i) % DEPTH).start()

    def z_all(n):
        others = zbuf.at[n, 1:DEPTH]
        return remote(others, others, z_send.at[n], z_recv.at[n], partner, zed)

    def peak_z_start(h):
        for i in range(1, DEPTH):
            remote(pz.at[h, 0], pz.at[h, i], pkz_send.at[h], pkz_recv.at[h], wide, (zed + i) % DEPTH).start()

    def peak_z_all(h):
        others = pz.at[h, 1:DEPTH]
        return remote(others, others, pkz_send.at[h], pkz_recv.at[h], partner, zed)

    def sum_start(n):
        core_out(n).start()
        if n < 2:
            pcore[n, 0] = jnp.max(peak[n], axis=0, keepdims=True)
            peak_core(n).start()

    def sum_core(n):
        core_out(n).wait_recv()
        psum[n] = pacc[n, :, core] + rcore[n]
        over_plane(plane_out(n), start)
        if n < 2:
            peak_core(n).wait_recv()
            pplane[n, 0] = jnp.maximum(pcore[n, 0], pcore[n, 1])
            over_plane(peak_plane(n), start)

    def sum_plane(n):
        plane_all(n).wait_recv()
        total = psum[n, chip]
        for i in range(1, PLANE):
            total = total + rplane[n, i]
        zbuf[n, zed] = total
        z_start(n)
        if n < 2:
            peak_plane_all(n).wait_recv()
            top = pplane[n, 0]
            for i in range(1, PLANE):
                top = jnp.maximum(top, pplane[n, i])
            pz[n, 0] = top
            peak_z_start(n)

    def sum_z(n):
        h = n % 2
        lanes = slice(h * HALF, (h + 1) * HALF)
        z_all(n).wait_recv()
        total = weight * (((zbuf[n, 0] + zbuf[n, 1]) + zbuf[n, 2]) + zbuf[n, 3])
        if n < 2:
            peak_z_all(n).wait_recv()
            top = jnp.maximum(jnp.maximum(pz[n, 0], pz[n, 1]), jnp.maximum(pz[n, 2], pz[n, 3]))
            step = STEP_LIMIT / (1.0 + top)
            step_out[:, lanes] = jnp.broadcast_to(step, (16, HALF))
            rate_one[:, lanes] = total
            cbuf[2 + h, chip, core] = coeffs[:, lanes] + step * total
            gather_start(2 + h)
        else:
            rate_two[:, lanes] = total

    def split_into(values, at):
        high, low = halves(values)
        bt[at:at + values.shape[0], 0:MODES] = high
        bt[at:at + values.shape[0], MODES:2 * MODES] = low

    def rims():
        halo_all(4).wait_recv()
        for k, at in ((0, 0), (1, ROWS + 1)):
            for part in range(2):
                split_into(halo_rows[k, part * 128:(part + 1) * 128, :], at * COLS + part * 128)

    nothing = lambda: None
    halo_all(5).wait_recv()
    for k in range(2):
        split_into(halo_cols[k].reshape(ROWS, MODES), EXT + 16 * k)
    gather_done(0)
    set_coeffs(0)
    section_of(0, 0, nothing, ((5, lambda: gather_plane(1)),), rims)
    sum_start(0)
    gather_done(1)
    set_coeffs(1)
    section_of(0, 1, lambda: sum_core(0), ((3, lambda: sum_plane(0)),), nothing)
    sum_start(1)
    sum_z(0)
    sum_core(1)
    gather_plane(2)
    sum_plane(1)
    gather_done(2)
    set_coeffs(2)
    section_of(1, 0, nothing, ((1, lambda: sum_z(1)),), lambda: gather_plane(3))
    sum_start(2)
    gather_done(3)
    set_coeffs(3)
    section_of(1, 1, nothing, ((0, lambda: sum_core(2)), (5, lambda: sum_plane(2))), nothing)
    sum_start(3)
    sum_core(3)
    sum_z(2)
    sum_plane(3)
    sum_z(3)

    for k in range(6):
        halo_all(k).wait_send()
    for g in range(4):
        for sent in (gather_all(g), share(g, core), core_out(g), plane_all(g), z_all(g)):
            sent.wait_send()
    for h in range(2):
        for sent in (peak_core(h), peak_plane_all(h), peak_z_all(h)):
            sent.wait_send()


def per_device(weight, coeffs, pod_basis, mean_field, velocity, diffusivity, reaction):
    vmem = lambda *shape: pltpu.VMEM(shape, F32)
    narrow = lambda *shape: pltpu.VMEM(shape, BF16)
    dma = lambda *shape: pltpu.SemaphoreType.DMA(shape)
    whole = pl.BlockSpec(memory_space=pltpu.VMEM)
    scratch = [
        vmem(16, TRAJ), vmem(ROWS, COLS), vmem(2, ROWS, COLS), vmem(ROWS, COLS), vmem(ROWS, COLS),
        vmem(ROWS, MODES, COLS),
        narrow(EXT + 32, 2 * MODES),
        narrow(ROWS, MODES, 2 * COLS),
        vmem(ROWS, COLS, 128),
        vmem(6, ROWS, COLS, 128),
        vmem(EXT + 32, 128),
        vmem(2, ROWS + 2, ROWPAD, 128),
        narrow(COLS, HALF),
        narrow(COLS, HALF),
        narrow(COLS, HALF),
        narrow(COLS, HALF),
        narrow(MODES, HALF),
        narrow(MODES, HALF),
        vmem(4, PLANE, 2, 16, HALF),
        vmem(4, PLANE, 16, HALF),
        vmem(4, PLANE, 16, HALF),
        vmem(4, PLANE, 16, HALF),
        vmem(4, DEPTH, 16, HALF),
        vmem(4, PLANE, 2, 16, HALF),
        vmem(2, COLS, MODES),
        vmem(2, COLS, MODES),
        vmem(2, ROWS, 1, MODES),
        vmem(2, ROWS, 1, MODES),
        vmem(2, 8, COLS),
        vmem(2, 8, COLS),
        vmem(2, ROWS, 128),
        vmem(2, ROWS, 128),
        vmem(2 * ROWS, 8, COLS),
        vmem(2, 8, HALF),
        vmem(2, 2, 1, HALF),
        vmem(2, PLANE, 1, HALF),
        vmem(2, DEPTH, 1, HALF),
        dma(5), dma(4),
        dma(4), dma(4), dma(4), dma(4),
        dma(6), dma(6), dma(4), dma(4),
        dma(4), dma(4), dma(4), dma(4),
        dma(2), dma(2), dma(2), dma(2), dma(2), dma(2),
    ]
    out = jax.ShapeDtypeStruct((16, TRAJ), F32)
    rate_one, rate_two, step_size = pl.pallas_call(
        functools.partial(kernel, weight),
        out_shape=(out, out, out),
        in_specs=[pl.BlockSpec(memory_space=pl.ANY)] * 6,
        out_specs=(whole, whole, whole),
        scratch_shapes=scratch,
        compiler_params=pltpu.CompilerParams(
            collective_id=0, has_side_effects=True, vmem_limit_bytes=67043328
        ),
    )(coeffs, pod_basis, mean_field, velocity, diffusivity, reaction)
    mean_rate = (rate_one + rate_two) * 0.5
    return coeffs + step_size * mean_rate, mean_rate


def solution(mesh):
    cells = ROWS * COLS * mesh.shape["wide"] * mesh.shape["col"]
    weight = math.sqrt(MODES / cells)
    placed = (
        P("wide", None),
        P(None, "wide", "col"),
        P("wide", "col"),
        P(None, "wide", "col"),
        P("wide", "col"),
        P("wide", "col"),
    )
    return jax.shard_map(
        functools.partial(per_device, weight),
        mesh=mesh,
        in_specs=placed,
        out_specs=(P("wide", None), P("wide", None)),
        check_vma=False,
    )
```
